256 devices in a mesh: seq: 128 (over y, x, z), head: 2 (over core).
Axes of the slice: x: 4, y: 4, z: 8, core: 2. Of those that a mesh axis runs over, the one named last changes fastest.
Arguments:
- tokens: bfloat16 [32768, 2048], P('seq'), may hold values from -6 to 6
- dest: int32 [32768], P('seq'), may hold values from 0 to 32767, as said below
- segment_ids: int32 [32768], P('seq'), may hold values from 0 to 255, never falling along the last dimension, each value on 1 to 1024 neighbouring positions
- gain: float32 [2048], replicated, may hold values from 0.1 to 1.9
- w_qkv: bfloat16 [2048, 3, 1024], P(None, None, 'head')
- w_out: bfloat16 [1024, 2048], P('head'), may hold values from -0.1875 to 0.1875
Outputs:
- layer_out: bfloat16 [32768, 2048], P('seq', 'head')
The draws below stay inside these ranges and needn't reach their ends.
Inputs may be any that keep to these rules, and one draw needn't show every extreme that they name: dest is a permutation of the sequence positions; the rows of one shard send exactly 2 rows to each shard's block of 256 positions.
All inputs are finite; a program needn't handle non-finite values.
Results may differ from the reference program's by a relative error of at most 0.017.
The reference program's roundings to bfloat16 on the way (of `normed`, `placed`, `qkv`, `fine_weights` and `attn`) count: a program that leaves them out, or rounds other values in their place, can miss the bound.
Values may be sent and summed in bfloat16 or wider, within the bound.
A program may use at most 128 MiB of HBM per device.

```python
import math
import jax
import jax.numpy as jnp
import numpy as np
from jax import lax

D = 2048
HEADS = 8
DH = 128
TOK_DEV = 256
POOL = 16
LEVELS = 4
TOKENS = 32768
DOCS = 256
N_SEQ = 128


def draw_dest(key, part):
    own_key = jax.random.fold_in(key, 101)
    peer_rows = TOK_DEV // N_SEQ
    first_key, second_key = jax.random.split(own_key)
    inbox = jax.vmap(lambda sub: jax.random.permutation(sub, TOK_DEV))(jax.random.split(first_key, N_SEQ))
    slots = jnp.arange(TOK_DEV, dtype=jnp.int32)
    target = slots // peer_rows
    within = slots % peer_rows
    owners = jnp.arange(N_SEQ, dtype=jnp.int32)[:, None]
    base = target[None, :] * TOK_DEV + inbox[target[None, :], owners * peer_rows + within[None, :]]
    shuffle = jax.vmap(lambda sub: jax.random.permutation(sub, TOK_DEV))(jax.random.split(second_key, N_SEQ))
    return jnp.take_along_axis(base, shuffle, axis=1).reshape(TOKENS).astype(jnp.int32)


def draw_w_qkv(key, part):
    own_key = jax.random.fold_in(key, 202)
    base_key = jax.random.fold_in(own_key, 0)
    shape = (D, 3, HEADS * DH)
    base = jax.random.normal(base_key, shape, jnp.float32)
    return (base * D ** (-0.5)).astype(jnp.bfloat16)


def block_levels(key, extent, cuts, low, top_value):
    def one(axis_at, shards_of):
        draws = jax.random.uniform(jax.random.fold_in(jax.random.fold_in(key, 6), axis_at), (shards_of,), jnp.float32, low / len(cuts), top_value / len(cuts))
        return jnp.repeat(jnp.exp(draws), extent[axis_at] // shards_of).reshape((-1,) + (1,) * (len(extent) - axis_at - 1))

    level = one(*cuts[0])
    for cut in cuts[1:]:
        level = level * one(*cut)
    return level


def length_profile(amount, total, bound, lean):
    loads = [(1 << 20) // math.isqrt(rank ** lean) + 1 for rank in range(2, amount + 1)]
    rest, counts = total - bound - (amount - 1), [1] * (amount - 1)
    while rest > 0:
        free = [i for i in range(amount - 1) if counts[i] < bound]
        pool, remaining = sum([loads[i] for i in free]), rest
        for i in free:
            more = min(bound - counts[i], max(1, remaining * loads[i] // pool), rest)
            counts[i] = counts[i] + more
            rest = rest - more
    return np.array([bound] + counts)


def uneven(key, number_of, total, reach, lean):
    if number_of == 2:
        one = jax.random.randint(key, (), max(1, total - reach), min(reach, total - 1) + 1)
        return jnp.stack([one, total - one])
    lengths = jnp.asarray(length_profile(number_of, total, reach, lean), jnp.int32)
    twos = (number_of - 1) // 2
    donor, receiver = lengths[1:1 + 2 * twos:2], lengths[2:2 + 2 * twos:2]
    margin = jnp.minimum(donor - 1, reach - receiver)
    shifted = jax.random.randint(jax.random.fold_in(key, 1), (twos,), 0, 1 << 20) % (margin + 1)
    lengths = lengths.at[1:1 + 2 * twos:2].set(donor - shifted).at[2:2 + 2 * twos:2].set(receiver + shifted)
    return lengths[jax.random.permutation(jax.random.fold_in(key, 2), number_of)]


def gaussian(key, dims, spread, most, cuts=(), kind=jnp.bfloat16):
    factor_of = block_levels(key, dims, cuts, -0.22, 0.18) if cuts else 1.0
    entries = jax.random.normal(key, dims, jnp.float32) * spread * factor_of
    return jnp.minimum(jnp.maximum(entries, -most), most).astype(kind)


def setup_inputs(seed: int = 0) -> dict:
    seeds = jax.random.split(jax.random.key(seed), 7)
    return {
        "tokens": gaussian(seeds[0], (TOKENS, D), 1.0, 6.0, ((0, 128),)),
        "dest": draw_dest(jax.random.fold_in(seeds[6], 71), 0),
        "segment_ids": jnp.searchsorted(jnp.cumsum(uneven(seeds[2], DOCS, TOKENS, 4 * TOK_DEV, 2)), jnp.arange(TOKENS), side="right").astype(jnp.int32),
        "gain": jnp.clip(1.0 + 0.18 * jax.random.normal(seeds[3], (D,), jnp.float32), 0.1, 1.9),
        "w_qkv": draw_w_qkv(jax.random.fold_in(seeds[6], 71), 0),
        "w_out": gaussian(seeds[5], (HEADS * DH, D), (HEADS * DH) ** -0.5, 0.1875, ((0, 2),)),
    }


def rms_norm(rows_in, gain):
    values = rows_in.astype(jnp.float32)
    scaled = values * lax.rsqrt(lax.optimization_barrier(jnp.mean(values * values, axis=-1, keepdims=True)) + 1e-05) * gain
    return scaled.astype(jnp.bfloat16)

def reference(tokens, dest, segment_ids, gain, w_qkv, w_out):
    shard_count = N_SEQ
    row_count = TOK_DEV
    pooled_count = row_count // POOL
    normed = rms_norm(tokens, gain)
    placed = jnp.zeros_like(normed).at[dest].set(normed)
    qkv = jnp.dot(placed, w_qkv.reshape(D, 3 * HEADS * DH), preferred_element_type=jnp.float32).astype(jnp.bfloat16)
    qkv = qkv.reshape(TOKENS, 3, HEADS, DH)
    queries = qkv[:, 0]
    keys = qkv[:, 1]
    values = qkv[:, 2]
    key_pool = keys.astype(jnp.float32).reshape(shard_count, pooled_count, POOL, HEADS, DH).mean(2)
    value_pool = values.astype(jnp.float32).reshape(shard_count, pooled_count, POOL, HEADS, DH).mean(2)
    shard_ids = jnp.arange(shard_count, dtype=jnp.int32)
    coarse_keys = []
    coarse_values = []
    offsets = []
    for level in range(LEVELS):
        partner = jnp.bitwise_xor(jnp.right_shift(shard_ids, level), 1)
        coarse_keys.append(key_pool[partner])
        coarse_values.append(value_pool[partner])
        offsets.append(jnp.full((pooled_count,), jnp.log(float(POOL * 2 ** level)), jnp.float32))
        groups = key_pool.shape[0] // 2
        key_pool = key_pool.reshape(groups, pooled_count, 2, HEADS, DH).mean(2)
        value_pool = value_pool.reshape(groups, pooled_count, 2, HEADS, DH).mean(2)
    coarse_keys = jnp.concatenate(coarse_keys, axis=1)
    coarse_values = jnp.concatenate(coarse_values, axis=1)
    level_bias = jnp.concatenate(offsets)
    padded_keys = jnp.pad(keys, ((row_count, row_count), (0, 0), (0, 0)))
    padded_values = jnp.pad(values, ((row_count, row_count), (0, 0), (0, 0)))
    padded_ids = jnp.pad(segment_ids, (row_count, row_count), constant_values=-1)
    score_scale = DH ** (-0.5)

    def one_shard(shard):
        start = (shard * row_count).astype(jnp.int32)
        query_block = lax.dynamic_slice_in_dim(queries, start, row_count, 0).astype(jnp.float32)
        own_ids = lax.dynamic_slice_in_dim(segment_ids, start, row_count, 0)
        near_keys = lax.dynamic_slice_in_dim(padded_keys, start, 3 * row_count, 0).astype(jnp.float32)
        near_values = lax.dynamic_slice_in_dim(padded_values, start, 3 * row_count, 0).astype(jnp.float32)
        near_ids = lax.dynamic_slice_in_dim(padded_ids, start, 3 * row_count, 0)
        fine = jnp.einsum('thd,khd->htk', query_block, near_keys) * score_scale
        same_doc = own_ids[:, None] == near_ids[None, :]
        fine = jnp.where(same_doc[None], fine, -jnp.inf)
        far_keys = coarse_keys[shard]
        far_values = coarse_values[shard]
        coarse = jnp.einsum('thd,khd->htk', query_block, far_keys, precision=lax.Precision.HIGHEST) * score_scale + level_bias
        top_score = jnp.maximum(lax.optimization_barrier(jnp.max(fine, axis=-1)), lax.optimization_barrier(jnp.max(coarse, axis=-1)))
        fine_weights = jnp.exp(fine - top_score[..., None])
        coarse_weights = jnp.exp(coarse - top_score[..., None])
        denominator = lax.optimization_barrier(jnp.sum(fine_weights, axis=-1)) + lax.optimization_barrier(jnp.sum(coarse_weights, axis=-1))
        rounded = fine_weights.astype(jnp.bfloat16).astype(jnp.float32)
        numerator = jnp.einsum('htk,khd->thd', rounded, near_values)
        numerator = numerator + jnp.einsum('htk,khd->thd', coarse_weights, far_values, precision=lax.Precision.HIGHEST)
        attn = (numerator / jnp.transpose(denominator)[..., None]).astype(jnp.bfloat16).reshape(row_count, HEADS * DH)
        return jnp.dot(attn, w_out, preferred_element_type=jnp.float32).astype(jnp.bfloat16)
    outputs = lax.map(one_shard, shard_ids)
    return outputs.reshape(TOKENS, D)
```

```python
import functools
import math

import jax
import jax.numpy as jnp
from jax import lax
from jax.experimental import pallas as pl
from jax.experimental.pallas import tpu as pltpu
from jax.sharding import PartitionSpec as P

MESH = pl.DeviceIdType.MESH
F32 = jnp.float32
BF16 = jnp.bfloat16
NX, NY, NZ = 4, 4, 8
NXY = NX * NY
SHARDS = NXY * NZ
ROWS = 256
WIDTH = 2048
DH = 128
GROUP = 512
HEADS = 4
CHUNKS = WIDTH // 128
SCORE = DH ** (-0.5) * math.log2(math.e)
Z_ORDER = (4, 3, 5, 2, 6, 1, 7, 0)


def iota(shape, dim):
    return lax.broadcasted_iota(jnp.int32, shape, dim)


def mm(a, b):
    return jnp.dot(a, b, preferred_element_type=F32)


def mm_nt(a, b):
    return lax.dot_general(a, b, (((1,), (1,)), ((), ())), preferred_element_type=F32)


def layer(
    tok_hbm, dest_ref, seg_ref, gain_ref, wqkv_hbm, wout_hbm, out_ref,
    tok, wqkv, wo_own, wo_sib, stage, send, recv, recv_sib, xs,
    posa_src, posa, posb_src, posb, place, pool,
    k_own, v_own, q_raw, q_own, ids_src, ids_halo, k_halo, v_halo,
    crs_src, crs, bias, top, tot, acc, prob, at_own, at_sib,
    load_sem, row_send, row_recv, sib_send, sib_recv,
    pos_sem, ids_sem, k_send, k_recv, v_send, v_recv, crs_sem, wo_sem, at_sem,
):
    me = lax.axis_index("seq")
    core = lax.axis_index("head")
    other = 1 - core
    xy, z = me // NZ, me % NZ
    y, x = xy // NX, xy % NX
    left, right = (me + SHARDS - 1) % SHARDS, (me + 1) % SHARDS

    def remote(src, dst, send_sem, recv_sem, seq, head):
        return pltpu.make_async_remote_copy(
            src_ref=src, dst_ref=dst, send_sem=send_sem, recv_sem=recv_sem,
            device_id=(seq, head), device_id_type=MESH,
        )

    def drain(ref, sem):
        pltpu.make_async_copy(ref, ref, sem).wait()

    load_tok = pltpu.make_async_copy(tok_hbm, tok, load_sem.at[0])
    load_tok.start()
    load_w = [
        pltpu.make_async_copy(wqkv_hbm.at[part], wqkv.at[part], load_sem.at[1 + part])
        for part in range(3)
    ]
    for part in (1, 2, 0):
        load_w[part].start()
    load_wo = pltpu.make_async_copy(
        wout_hbm.at[:, pl.ds(pl.multiple_of(core * 1024, 1024), 1024)], wo_own, load_sem.at[4]
    )
    load_wo.start()

    barrier = pltpu.get_barrier_semaphore()

    def greet(i, carry):
        pl.semaphore_signal(
            barrier, inc=1, device_id=((me + 1 + i) % SHARDS, core), device_id_type=MESH
        )
        return carry

    lax.fori_loop(0, SHARDS - 1, greet, 0)
    pl.semaphore_signal(barrier, inc=1, device_id=(me, other), device_id_type=MESH)

    dest = dest_ref[...]
    shard = jnp.right_shift(dest, 8).astype(F32)
    slot = jnp.bitwise_and(dest, 255).astype(F32)
    by_lane = jnp.broadcast_to(shard, (ROWS, ROWS))
    by_row = by_lane.T
    earlier = (by_lane == by_row) & (iota((ROWS, ROWS), 0) < iota((ROWS, ROWS), 1))
    rank = jnp.sum(jnp.where(earlier, 1.0, 0.0), axis=0, keepdims=True)
    hit = iota((SHARDS, ROWS), 0).astype(F32) == shard
    mine = hit & (rank == core.astype(F32))
    pick = jnp.where(mine, 1.0, 0.0).astype(BF16)
    pair = iota((8, ROWS), 0).astype(F32) == rank
    slots = jnp.where(pair, slot, 0.0).astype(BF16)
    posa_src[...] = mm_nt(slots, jnp.where(hit, 1.0, 0.0).astype(BF16))
    load_tok.wait()
    gain = gain_ref[...]
    rows = mm(pick, tok[...])
    scale = lax.rsqrt(jnp.sum(rows * rows, axis=-1, keepdims=True) * (1.0 / WIDTH) + 1e-05)
    for j in range(CHUNKS):
        cols = slice(j * 128, (j + 1) * 128)
        stage[pl.ds(j, SHARDS, stride=CHUNKS), :] = rows[:, cols] * scale * gain[:, cols]
    send[...] = stage[...].reshape(SHARDS, CHUNKS, 128).astype(BF16)

    pl.semaphore_wait(barrier, SHARDS)

    posa[pl.ds(pl.multiple_of(z * 8, 8), 8), :] = posa_src[...]
    for o in range(1, NZ):
        remote(
            posa_src, posa.at[pl.ds(pl.multiple_of(z * 8, 8), 8)], pos_sem.at[0], pos_sem.at[1],
            xy * NZ + (z + o) % NZ, core,
        ).start()

    def offsets(i):
        return (i // NX + 1) % NX, (i % NX + 1) % NX

    def send_rows(i, skip_self):
        ox, oy = offsets(i)
        base = (((y + oy) % NY) * NX + (x + ox) % NX) * NZ
        for oz in Z_ORDER:
            if skip_self and oz == 0:
                continue
            peer = base + (z + oz) % NZ
            remote(
                send.at[peer], recv.at[me], row_send, row_recv.at[i], peer, core
            ).start()

    def send_loop(i, carry):
        send_rows(i, False)
        return carry

    lax.fori_loop(0, NXY - 1, send_loop, 0)
    send_rows(NXY - 1, True)
    pltpu.make_async_copy(send.at[me], recv.at[me], row_recv.at[NXY - 1]).start()

    remote(
        wout_hbm.at[:, pl.ds(pl.multiple_of(other * 1024, 1024), 1024)], wo_sib,
        wo_sem.at[0], wo_sem.at[1], me, other,
    ).start()

    drain(posa.at[pl.ds(0, 56)], pos_sem.at[1])
    for k in range(2):
        posb_src[k * 8:(k + 1) * 8, :] = posa[pl.ds(k, 8, stride=8), :]
    posb[pl.ds(pl.multiple_of(xy * 16, 16), 16), :] = posb_src[...]

    def send_pos(o, carry):
        remote(
            posb_src, posb.at[pl.ds(pl.multiple_of(xy * 16, 16), 16)], pos_sem.at[2],
            pos_sem.at[3], ((xy + o) % NXY) * NZ + z, core,
        ).start()
        return carry

    lax.fori_loop(1, NXY, send_pos, 0)
    drain(posb.at[pl.ds(0, 240)], pos_sem.at[3])
    table = posb[...].reshape(NXY, 16, 128)
    my_lane = jnp.where(iota((8, 128), 1) == me, 1.0, 0.0).astype(BF16)
    found = [
        mm_nt(my_lane, table[:, k * 8:(k + 1) * 8, :].reshape(SHARDS, 128).astype(BF16))
        for k in range(2)
    ]
    first = core == 0
    pos = jnp.concatenate(
        [jnp.where(first, found[0], found[1]), jnp.where(first, found[1], found[0])], axis=1
    )
    pos_row = pos[0:1, :]
    where_to = jnp.where(iota((ROWS, ROWS), 0).astype(F32) == pos_row, 1.0, 0.0).astype(BF16)
    place[...] = where_to
    seg = seg_ref[...].astype(F32)
    ids_src[...] = mm(jnp.broadcast_to(seg, (8, ROWS)).astype(BF16), where_to)
    for side, peer in ((1, left), (0, right)):
        remote(ids_src, ids_halo.at[side], ids_sem.at[0], ids_sem.at[1], peer, core).start()

    place_int = pos_row.astype(jnp.int32)
    line = iota((128, ROWS), 0)
    spread = jnp.broadcast_to(place_int, (128, ROWS))
    weights = jnp.zeros((128, ROWS), F32)
    start = 0
    for level in range(4):
        count = 16 >> level
        inside = (line >= start) & (line < start + HEADS * count)
        same = jnp.right_shift(spread, 4 + level) == (line - start) % count
        weights = jnp.where(inside & same, 1.0 / (16 << level), weights)
        start += HEADS * count
    pool[...] = weights.astype(BF16)

    own_col = jnp.broadcast_to(seg, (ROWS, ROWS)).T
    bias[:, 0:ROWS] = jnp.where(own_col == ids_src[0:1, :], 0.0, -jnp.inf)

    def share(i, carry):
        ox, oy = offsets(i)
        base = (((y + NY - oy) % NY) * NX + (x + NX - ox) % NX) * NZ
        block = pl.ds(base, NZ)
        drain(recv.at[block], row_recv.at[i])
        remote(recv.at[block], recv_sib.at[block], sib_send, sib_recv, me, other).start()
        return carry

    lax.fori_loop(0, NXY, share, 0)
    stage[...] = recv[...].astype(F32).reshape(SHARDS * CHUNKS, 128)
    for j in range(CHUNKS):
        xs[0:128, j * 128:(j + 1) * 128] = stage[pl.ds(j, SHARDS, stride=CHUNKS), :].astype(BF16)
    drain(recv_sib, sib_recv)
    stage[...] = recv_sib[...].astype(F32).reshape(SHARDS * CHUNKS, 128)
    for j in range(CHUNKS):
        xs[128:256, j * 128:(j + 1) * 128] = stage[pl.ds(j, SHARDS, stride=CHUNKS), :].astype(BF16)

    for part, own, halo, send_sem, recv_sem in (
        (1, k_own, k_halo, k_send, k_recv), (2, v_own, v_halo, v_send, v_recv)
    ):
        load_w[part].wait()
        for half in range(2):
            cols = slice(half * 256, (half + 1) * 256)
            own[half] = mm(xs[...], wqkv[part, :, cols]).astype(BF16)
            for side, peer in ((1, left), (0, right)):
                remote(
                    own.at[half], halo.at[side, half], send_sem, recv_sem.at[side, half], peer, core
                ).start()

    line = iota((128, 128), 0)
    head_of = jnp.where(
        line < 64, line // 16,
        jnp.where(line < 96, (line - 64) // 8, jnp.where(line < 112, (line - 96) // 4, (line - 112) // 2)),
    )
    for which, own in ((0, k_own), (1, v_own)):
        picked = jnp.zeros((128, 128), F32)
        for half in range(2):
            means = mm(pool[...], own[half])
            for sub in range(2):
                picked = jnp.where(
                    head_of == half * 2 + sub, means[:, sub * 128:(sub + 1) * 128], picked
                )
        crs_src[:, which * 128:(which + 1) * 128] = picked.astype(BF16)
    start = 0
    for level in range(4):
        size = 1 << level
        lines = 64 >> level
        group = me // size
        partner = group + 1 - 2 * (group % 2)
        for i in range(size):
            remote(
                crs_src.at[pl.ds(start, lines)],
                crs.at[pl.ds(pl.multiple_of(64 * level + (me % size) * lines, 8), lines)],
                crs_sem.at[0], crs_sem.at[1], partner * size + i, core,
            ).start()
        start += lines

    load_w[0].wait()
    for half in range(2):
        cols = slice(half * 256, (half + 1) * 256)
        q_raw[half] = mm(xs[...], wqkv[0, :, cols]).astype(BF16)
    for half in range(2):
        q_own[half] = mm(place[...], q_raw[half]).astype(BF16)

    def head(ref, h):
        return ref[h // 2, :, (h % 2) * 128:(h % 2 + 1) * 128]

    def fine(h, keys, mask):
        return mm_nt(head(q_own, h), keys) * SCORE + mask

    for h in range(HEADS):
        score = fine(h, head(k_own, h), bias[:, 0:ROWS])
        best = jnp.max(score, axis=-1, keepdims=True)
        weight = jnp.exp2(score - best)
        tot[h] = jnp.broadcast_to(jnp.sum(weight, axis=-1, keepdims=True), (ROWS, 128))
        top[h] = jnp.broadcast_to(best, (ROWS, 128))
        acc[h] = mm(weight.astype(BF16), head(v_own, h))

    drain(ids_halo, ids_sem.at[1])
    own_col = jnp.broadcast_to(seg, (ROWS, ROWS)).T
    edge = ((me > 0), (me < SHARDS - 1))
    for side in range(2):
        same = own_col == ids_halo[side][0:1, :]
        bias[:, (side + 1) * ROWS:(side + 2) * ROWS] = jnp.where(same & edge[side], 0.0, -jnp.inf)

    drain(crs, crs_sem.at[1])
    lane = iota((8, 256), 1)
    level_of = lane // 64
    holder = jnp.where(
        level_of == 0, (lane % 64) // 16,
        jnp.where(level_of == 1, (lane % 32) // 8, jnp.where(level_of == 2, (lane % 16) // 4, (lane % 8) // 2)),
    )
    lift = (level_of + 4).astype(F32)
    for h in range(HEADS):
        far_mask = jnp.where(holder == h, lift, -jnp.inf)[0:1, :]
        score = fine(h, crs[:, 0:128], far_mask)
        old = top[h][:, 0:1]
        best = jnp.maximum(old, jnp.max(score, axis=-1, keepdims=True))
        weight = jnp.exp2(score - best)
        fade = jnp.exp2(old - best)
        tot[h] = tot[h] * fade + jnp.sum(weight, axis=-1, keepdims=True)
        top[h] = jnp.broadcast_to(best, (ROWS, 128))
        acc[h] = acc[h] * fade + mm(weight.astype(BF16), crs[:, 128:256])

    for half in range(2):
        for side in range(2):
            drain(k_halo.at[side, half], k_recv.at[side, half])
        for h in (half * 2, half * 2 + 1):
            cols = slice((h % 2) * 128, (h % 2 + 1) * 128)
            scores = [
                fine(h, k_halo[side, half, :, cols], bias[:, (side + 1) * ROWS:(side + 2) * ROWS])
                for side in range(2)
            ]
            old = top[h][:, 0:1]
            best = old
            for score in scores:
                best = jnp.maximum(best, jnp.max(score, axis=-1, keepdims=True))
            fade = jnp.exp2(old - best)
            total = tot[h] * fade
            for side in range(2):
                weight = jnp.exp2(scores[side] - best)
                total = total + jnp.sum(weight, axis=-1, keepdims=True)
                prob[h, side] = weight.astype(BF16)
            tot[h] = total
            acc[h] = acc[h] * fade

    load_wo.wait()
    for half in range(2):
        for side in range(2):
            drain(v_halo.at[side, half], v_recv.at[side, half])
        for h in (half * 2, half * 2 + 1):
            cols = slice((h % 2) * 128, (h % 2 + 1) * 128)
            total = acc[h]
            for side in range(2):
                total = total + mm(prob[h, side], v_halo[side, half, :, cols])
            at_own[half, :, cols] = (total / tot[h]).astype(BF16)
        remote(
            at_own.at[half], at_sib.at[half], at_sem.at[0], at_sem.at[1 + half], me, other
        ).start()

    drain(wo_sib, wo_sem.at[1])
    for half in range(2):
        drain(at_sib.at[half], at_sem.at[1 + half])
    for part in range(4):
        cols = slice(part * 256, (part + 1) * 256)
        total = jnp.zeros((ROWS, 256), F32)
        for half in range(2):
            lines = slice(half * 256, (half + 1) * 256)
            total = total + mm(at_own[half], wo_own[lines, cols])
            total = total + mm(at_sib[half], wo_sib[lines, cols])
        out_ref[:, cols] = total.astype(BF16)

    drain(send.at[pl.ds(0, SHARDS - 1)], row_send)
    drain(posa.at[pl.ds(0, 56)], pos_sem.at[0])
    drain(posb.at[pl.ds(0, 240)], pos_sem.at[2])
    drain(ids_halo, ids_sem.at[0])
    drain(recv, sib_send)
    drain(k_halo, k_send)
    drain(v_halo, v_send)
    drain(crs, crs_sem.at[0])
    drain(wo_sib, wo_sem.at[0])
    drain(at_own, at_sem.at[0])


def shards(tokens, dest, segment_ids, gain, w_qkv, w_out):
    vmem = pl.BlockSpec(memory_space=pltpu.VMEM)
    hbm = pl.BlockSpec(memory_space=pl.ANY)
    dma = pltpu.SemaphoreType.DMA
    V = pltpu.VMEM
    return pl.pallas_call(
        layer,
        out_shape=jax.ShapeDtypeStruct((ROWS, 1024), BF16),
        in_specs=[hbm, vmem, vmem, vmem, hbm, hbm],
        out_specs=vmem,
        scratch_shapes=[
            V((ROWS, WIDTH), BF16), V((3, WIDTH, GROUP), BF16), V((GROUP, 1024), BF16),
            V((GROUP, 1024), BF16), V((SHARDS * CHUNKS, 128), F32), V((SHARDS, CHUNKS, 128), BF16),
            V((SHARDS, CHUNKS, 128), BF16), V((SHARDS, CHUNKS, 128), BF16), V((ROWS, WIDTH), BF16),
            V((8, 128), F32), V((64, 128), F32), V((16, 128), F32), V((256, 128), F32),
            V((ROWS, ROWS), BF16), V((128, ROWS), BF16),
            V((2, ROWS, 256), BF16), V((2, ROWS, 256), BF16), V((2, ROWS, 256), BF16),
            V((2, ROWS, 256), BF16), V((8, ROWS), F32), V((2, 8, ROWS), F32),
            V((2, 2, ROWS, 256), BF16), V((2, 2, ROWS, 256), BF16),
            V((128, 256), BF16), V((256, 256), BF16), V((ROWS, 3 * ROWS), F32),
            V((HEADS, ROWS, 128), F32), V((HEADS, ROWS, 128), F32), V((HEADS, ROWS, 128), F32),
            V((HEADS, 2, ROWS, ROWS), BF16), V((2, ROWS, 256), BF16), V((2, ROWS, 256), BF16),
            dma((5,)), dma, dma((NXY,)), dma, dma,
            dma((4,)), dma((2,)), dma, dma((2, 2)), dma, dma((2, 2)), dma((2,)), dma((2,)), dma((3,)),
        ],
        compiler_params=pltpu.CompilerParams(collective_id=0, has_side_effects=True),
    )(
        tokens, dest.reshape(1, ROWS), segment_ids.reshape(1, ROWS), gain.reshape(1, WIDTH),
        jnp.transpose(w_qkv, (1, 0, 2)), w_out,
    )


def solution(mesh):
    in_specs = (P("seq", None), P("seq"), P("seq"), P(), P(None, None, "head"), P("head", None))
    return jax.shard_map(
        shards, mesh=mesh, in_specs=in_specs, out_specs=P("seq", "head"), check_vma=False
    )
```

```python
import functools
import math

import jax
import jax.numpy as jnp
from jax import lax
from jax.experimental import pallas as pl
from jax.experimental.pallas import tpu as pltpu
from jax.sharding import PartitionSpec as P

MESH = pl.DeviceIdType.MESH
F32 = jnp.float32
BF16 = jnp.bfloat16
NX, NY, NZ = 4, 4, 8
NXY = NX * NY
SHARDS = NXY * NZ
ROWS = 256
WIDTH = 2048
DH = 128
GROUP = 512
HEADS = 4
CHUNKS = WIDTH // 128
SCORE = DH ** (-0.5) * math.log2(math.e)
WAVES = ((0,), (1, 7), (2, 6), (4,), (3, 5))
ORDER = tuple(oz for wave in WAVES for oz in wave)
EARLY = 4


def iota(shape, dim):
    return lax.broadcasted_iota(jnp.int32, shape, dim)


def mm(a, b):
    return jnp.dot(a, b, preferred_element_type=F32)


def mm_nt(a, b):
    return lax.dot_general(a, b, (((1,), (1,)), ((), ())), preferred_element_type=F32)


def layer(
    tok_hbm, dest_ref, seg_ref, gain_ref, wqkv_hbm, wout_hbm, out_ref,
    tok, wqkv, wo_own, wo_sib, stage, send, recv, recv_sib, xs,
    posa_src, posa, posb_src, posb, place, pool,
    k_own, v_own, q_raw, q_own, ids_src, ids_halo, k_halo, v_halo,
    crs_src, crs, line_up, far, bias, top, tot, acc, prob, at_own, at_sib,
    load_sem, row_send, row_recv, sib_send, sib_recv, go,
    pos_sem, ids_sem, k_send, k_recv, v_send, v_recv, crs_sem, wo_sem, at_sem,
):
    me = lax.axis_index("seq")
    core = lax.axis_index("head")
    other = 1 - core
    xy, z = me // NZ, me % NZ
    y, x = xy // NX, xy % NX
    left, right = (me + SHARDS - 1) % SHARDS, (me + 1) % SHARDS

    def remote(src, dst, send_sem, recv_sem, seq, head):
        return pltpu.make_async_remote_copy(
            src_ref=src, dst_ref=dst, send_sem=send_sem, recv_sem=recv_sem,
            device_id=(seq, head), device_id_type=MESH,
        )

    def drain(ref, sem):
        pltpu.make_async_copy(ref, ref, sem).wait()

    load_tok = pltpu.make_async_copy(tok_hbm, tok, load_sem.at[0])
    load_tok.start()
    load_w = [
        pltpu.make_async_copy(wqkv_hbm.at[part], wqkv.at[part], load_sem.at[1 + part])
        for part in range(3)
    ]
    for part in (1, 2, 0):
        load_w[part].start()
    load_wo = pltpu.make_async_copy(
        wout_hbm.at[:, pl.ds(pl.multiple_of(core * 1024, 1024), 1024)], wo_own, load_sem.at[4]
    )
    load_wo.start()

    barrier = pltpu.get_barrier_semaphore()
    for o in range(1, NZ):
        pl.semaphore_signal(
            barrier, inc=1, device_id=(xy * NZ + (z + o) % NZ, core), device_id_type=MESH
        )

    def greet(o, carry):
        pl.semaphore_signal(
            barrier, inc=1, device_id=(((xy + o) % NXY) * NZ + z, core), device_id_type=MESH
        )
        return carry

    lax.fori_loop(1, NXY, greet, 0)
    pl.semaphore_signal(barrier, inc=1, device_id=(me, other), device_id_type=MESH)

    dest = dest_ref[...]
    shard = jnp.right_shift(dest, 8).astype(F32)
    slot = jnp.bitwise_and(dest, 255).astype(F32)
    by_lane = jnp.broadcast_to(shard, (ROWS, ROWS))
    by_row = by_lane.T
    earlier = (by_lane == by_row) & (iota((ROWS, ROWS), 0) < iota((ROWS, ROWS), 1))
    rank = jnp.sum(jnp.where(earlier, 1.0, 0.0), axis=0, keepdims=True)
    hit = iota((SHARDS, ROWS), 0).astype(F32) == shard
    mine = hit & (rank == core.astype(F32))
    pick = jnp.where(mine, 1.0, 0.0).astype(BF16)
    pair = iota((8, ROWS), 0).astype(F32) == rank
    slots = jnp.where(pair, slot, 0.0).astype(BF16)
    posa_src[...] = mm_nt(slots, jnp.where(hit, 1.0, 0.0).astype(BF16))[0:2, :]
    load_tok.wait()
    gain = gain_ref[...]
    rows = mm(pick, tok[...])
    scale = lax.rsqrt(jnp.sum(rows * rows, axis=-1, keepdims=True) * (1.0 / WIDTH) + 1e-05)
    for j in range(CHUNKS):
        cols = slice(j * 128, (j + 1) * 128)
        stage[pl.ds(j, SHARDS, stride=CHUNKS), :] = rows[:, cols] * scale * gain[:, cols]
    send[...] = stage[...].reshape(SHARDS, CHUNKS, 128).astype(BF16)

    pl.semaphore_wait(barrier, NZ - 1 + NXY)
    for o in range(1, NZ):
        pl.semaphore_signal(
            go.at[NZ - o], inc=1, device_id=(xy * NZ + (z + o) % NZ, core), device_id_type=MESH
        )

    posa[z] = posa_src[...]
    for o in range(1, NZ):
        remote(
            posa_src, posa.at[z], pos_sem.at[0], pos_sem.at[1], xy * NZ + (z + o) % NZ, core,
        ).start()

    def send_rows(first, wave):
        def body(i, carry):
            at = ((y + i // NX) % NY) * NX + (x + i % NX) % NX
            for oz in wave:
                group = ORDER.index(oz)
                peer = at * NZ + (z + oz) % NZ
                remote(
                    send.at[peer], recv.at[group * NXY + xy], row_send, row_recv.at[group],
                    peer, core,
                ).start()
            return carry

        lax.fori_loop(first, NXY, body, 0)

    pltpu.make_async_copy(send.at[me], recv.at[xy], row_recv.at[0]).start()
    send_rows(1, WAVES[0])
    for number, wave in enumerate(WAVES[1:]):
        for oz in wave:
            pl.semaphore_wait(go.at[oz], 1)
        send_rows(0, wave)
        if number == 1:
            drain(posa.at[pl.ds(0, NZ - 1)], pos_sem.at[1])
            for oz in range(NZ):
                for k in range(2):
                    posb_src[k * NZ + oz:k * NZ + oz + 1, :] = posa[oz, k:k + 1, :]
            posb[pl.ds(pl.multiple_of(xy * 16, 16), 16), :] = posb_src[...]

            def send_pos(o, carry):
                remote(
                    posb_src, posb.at[pl.ds(pl.multiple_of(xy * 16, 16), 16)], pos_sem.at[2],
                    pos_sem.at[3], ((xy + o) % NXY) * NZ + z, core,
                ).start()
                return carry

            lax.fori_loop(1, NXY, send_pos, 0)

    def unpack(group, landed, line):
        part = pl.ds(group * NXY * CHUNKS, NXY * CHUNKS)
        stage[part, :] = (
            landed[group * NXY:(group + 1) * NXY].astype(F32).reshape(NXY * CHUNKS, 128)
        )
        for j in range(CHUNKS):
            xs[line:line + NXY, j * 128:(j + 1) * 128] = (
                stage[pl.ds(group * NXY * CHUNKS + j, NXY, stride=CHUNKS), :].astype(BF16)
            )

    def collect(first):
        base = (first // EARLY) * 128
        for group in range(first, first + EARLY):
            block = pl.ds(group * NXY, NXY)
            drain(recv.at[block], row_recv.at[group])
            remote(
                recv.at[block], recv_sib.at[block], sib_send, sib_recv.at[group], me, other
            ).start()
            unpack(group, recv, base + (group - first) * NXY)
        for group in range(first, first + EARLY):
            drain(recv_sib.at[pl.ds(group * NXY, NXY)], sib_recv.at[group])
            unpack(group, recv_sib, base + 64 + (group - first) * NXY)

    def project(part, own, half):
        lines = slice(half * 128, (half + 1) * 128)
        own[lines, :] = mm(xs[lines, :], wqkv[part]).astype(BF16)

    def send_halo(own, halo, half, send_sem, recv_sem):
        lines = pl.ds(half * 128, 128)
        for side, peer in ((1, left), (0, right)):
            remote(
                own.at[lines], halo.at[side, lines], send_sem, recv_sem.at[side, half], peer, core
            ).start()

    collect(0)
    load_w[1].wait()
    load_w[2].wait()
    project(1, k_own, 0)
    send_halo(k_own, k_halo, 0, k_send, k_recv)
    project(2, v_own, 0)
    send_halo(v_own, v_halo, 0, v_send, v_recv)

    drain(posb.at[pl.ds(0, 240)], pos_sem.at[3])
    pieces = []
    for first in (0, EARLY):
        for who in (core, other):
            for oz in ORDER[first:first + EARLY]:
                pieces.append(posb[pl.ds(who * NZ + (z + NZ - oz) % NZ, NXY, stride=16), :])
    table = jnp.concatenate(pieces, axis=0).astype(BF16)
    my_lane = jnp.where(iota((8, 128), 1) == me, 1.0, 0.0).astype(BF16)
    pos_row = mm_nt(my_lane, table)[0:1, :]
    where_to = jnp.where(iota((ROWS, ROWS), 0).astype(F32) == pos_row, 1.0, 0.0).astype(BF16)
    place[...] = where_to
    seg = seg_ref[...].astype(F32)
    ids_src[...] = mm(jnp.broadcast_to(seg, (8, ROWS)).astype(BF16), where_to)
    for side, peer in ((1, left), (0, right)):
        remote(ids_src, ids_halo.at[side], ids_sem.at[0], ids_sem.at[1], peer, core).start()

    place_int = pos_row.astype(jnp.int32)
    line = iota((128, ROWS), 0)
    spread = jnp.broadcast_to(place_int, (128, ROWS))
    weights = jnp.zeros((128, ROWS), F32)
    start = 0
    for level in range(4):
        count = 16 >> level
        inside = (line >= start) & (line < start + HEADS * count)
        same = jnp.right_shift(spread, 4 + level) == (line - start) % count
        weights = jnp.where(inside & same, 1.0 / (16 << level), weights)
        start += HEADS * count
    pool[...] = weights.astype(BF16)

    line = iota((256, 256), 0)
    head_at, unit = line // 64, line % 16
    level_at = (line % 64) // 16
    origin = jnp.where(
        level_at == 0, head_at * 16 + unit,
        jnp.where(
            level_at == 1, 64 + (unit // 8) * 32 + head_at * 8 + unit % 8,
            jnp.where(
                level_at == 2, 128 + (unit // 4) * 16 + head_at * 4 + unit % 4,
                192 + (unit // 2) * 8 + head_at * 2 + unit % 2,
            ),
        ),
    )
    line_up[...] = jnp.where(iota((256, 256), 1) == origin, 1.0, 0.0).astype(BF16)

    own_col = jnp.broadcast_to(seg, (ROWS, ROWS)).T
    bias[:, 0:ROWS] = jnp.where(own_col == ids_src[0:1, :], 0.0, -jnp.inf)

    collect(EARLY)
    project(1, k_own, 1)
    send_halo(k_own, k_halo, 1, k_send, k_recv)
    project(2, v_own, 1)

    line = iota((128, 128), 0)
    head_of = jnp.where(
        line < 64, line // 16,
        jnp.where(line < 96, (line - 64) // 8, jnp.where(line < 112, (line - 96) // 4, (line - 112) // 2)),
    )
    for which, own in ((0, k_own), (1, v_own)):
        picked = jnp.zeros((128, 128), F32)
        for half in range(2):
            means = mm(pool[...], own[:, half * 256:(half + 1) * 256])
            for sub in range(2):
                picked = jnp.where(
                    head_of == half * 2 + sub, means[:, sub * 128:(sub + 1) * 128], picked
                )
        crs_src[:, which * 128:(which + 1) * 128] = picked.astype(BF16)
    start = 0
    for level in range(4):
        size = 1 << level
        lines = 64 >> level
        group = me // size
        partner = group + 1 - 2 * (group % 2)
        for i in range(size):
            remote(
                crs_src.at[pl.ds(start, lines)],
                crs.at[pl.ds(pl.multiple_of(64 * level + (me % size) * lines, 8), lines)],
                crs_sem.at[0], crs_sem.at[1], partner * size + i, core,
            ).start()
        start += lines
    send_halo(v_own, v_halo, 1, v_send, v_recv)
    remote(
        wout_hbm.at[:, pl.ds(pl.multiple_of(other * 1024, 1024), 1024)], wo_sib,
        wo_sem.at[0], wo_sem.at[1], me, other,
    ).start()

    load_w[0].wait()
    for half in range(2):
        cols = slice(half * 256, (half + 1) * 256)
        q_raw[half] = mm(xs[...], wqkv[0, :, cols]).astype(BF16)
    for half in range(2):
        q_own[half] = mm(place[...], q_raw[half]).astype(BF16)

    def head(ref, h):
        return ref[:, h * 128:(h + 1) * 128]

    def fine(h, keys, mask):
        return mm_nt(q_own[h // 2, :, (h % 2) * 128:(h % 2 + 1) * 128], keys) * SCORE + mask

    for h in range(HEADS):
        score = fine(h, head(k_own, h), bias[:, 0:ROWS])
        best = jnp.max(score, axis=-1, keepdims=True)
        weight = jnp.exp2(score - best)
        tot[h] = jnp.broadcast_to(jnp.sum(weight, axis=-1, keepdims=True), (ROWS, 128))
        top[h] = jnp.broadcast_to(best, (ROWS, 128))
        acc[h] = mm(weight.astype(BF16), head(v_own, h))

    drain(ids_halo, ids_sem.at[1])
    own_col = jnp.broadcast_to(seg, (ROWS, ROWS)).T
    edge = ((me > 0), (me < SHARDS - 1))
    for side in range(2):
        same = own_col == ids_halo[side][0:1, :]
        bias[:, (side + 1) * ROWS:(side + 2) * ROWS] = jnp.where(same & edge[side], 0.0, -jnp.inf)

    for half in range(2):
        for side in range(2):
            drain(k_halo.at[side, pl.ds(half * 128, 128)], k_recv.at[side, half])
    drain(crs, crs_sem.at[1])
    far[...] = mm(line_up[...], crs[...]).astype(BF16)
    lift = (iota((8, 64), 1) // 16 + 4).astype(F32)[0:1, :]

    for h in range(HEADS):
        scores = [
            fine(h, head(k_halo.at[side], h), bias[:, (side + 1) * ROWS:(side + 2) * ROWS])
            for side in range(2)
        ]
        scores.append(fine(h, far[h * 64:(h + 1) * 64, 0:128], lift))
        old = top[h][:, 0:1]
        best = old
        for score in scores:
            best = jnp.maximum(best, jnp.max(score, axis=-1, keepdims=True))
        fade = jnp.exp2(old - best)
        weight = jnp.exp2(scores[2] - best)
        total = tot[h] * fade + jnp.sum(weight, axis=-1, keepdims=True)
        acc[h] = acc[h] * fade + mm(weight.astype(BF16), far[h * 64:(h + 1) * 64, 128:256])
        for side in range(2):
            weight = jnp.exp2(scores[side] - best)
            total = total + jnp.sum(weight, axis=-1, keepdims=True)
            prob[h, side] = weight.astype(BF16)
        tot[h] = total

    load_wo.wait()
    for half in range(2):
        for side in range(2):
            drain(v_halo.at[side, pl.ds(half * 128, 128)], v_recv.at[side, half])
    for half in range(2):
        for h in (half * 2, half * 2 + 1):
            total = acc[h]
            for side in range(2):
                total = total + mm(prob[h, side], head(v_halo.at[side], h))
            at_own[half, :, (h % 2) * 128:(h % 2 + 1) * 128] = (total / tot[h]).astype(BF16)
        remote(
            at_own.at[half], at_sib.at[half], at_sem.at[0], at_sem.at[1 + half], me, other
        ).start()

    drain(wo_sib, wo_sem.at[1])
    for half in range(2):
        drain(at_sib.at[half], at_sem.at[1 + half])
    for part in range(4):
        cols = slice(part * 256, (part + 1) * 256)
        total = jnp.zeros((ROWS, 256), F32)
        for half in range(2):
            lines = slice(half * 256, (half + 1) * 256)
            total = total + mm(at_own[half], wo_own[lines, cols])
            total = total + mm(at_sib[half], wo_sib[lines, cols])
        out_ref[:, cols] = total.astype(BF16)

    drain(send.at[pl.ds(0, SHARDS - 1)], row_send)
    drain(posa.at[pl.ds(0, NZ - 1)], pos_sem.at[0])
    drain(posb.at[pl.ds(0, 240)], pos_sem.at[2])
    drain(ids_halo, ids_sem.at[0])
    drain(recv, sib_send)
    drain(k_halo, k_send)
    drain(v_halo, v_send)
    drain(crs, crs_sem.at[0])
    drain(wo_sib, wo_sem.at[0])
    drain(at_own, at_sem.at[0])


def shards(tokens, dest, segment_ids, gain, w_qkv, w_out):
    vmem = pl.BlockSpec(memory_space=pltpu.VMEM)
    hbm = pl.BlockSpec(memory_space=pl.ANY)
    dma = pltpu.SemaphoreType.DMA
    V = pltpu.VMEM
    return pl.pallas_call(
        layer,
        out_shape=jax.ShapeDtypeStruct((ROWS, 1024), BF16),
        in_specs=[hbm, vmem, vmem, vmem, hbm, hbm],
        out_specs=vmem,
        scratch_shapes=[
            V((ROWS, WIDTH), BF16), V((3, WIDTH, GROUP), BF16), V((GROUP, 1024), BF16),
            V((GROUP, 1024), BF16), V((SHARDS * CHUNKS, 128), F32), V((SHARDS, CHUNKS, 128), BF16),
            V((SHARDS, CHUNKS, 128), BF16), V((SHARDS, CHUNKS, 128), BF16), V((ROWS, WIDTH), BF16),
            V((2, 128), F32), V((NZ, 2, 128), F32), V((16, 128), F32), V((256, 128), F32),
            V((ROWS, ROWS), BF16), V((128, ROWS), BF16),
            V((ROWS, GROUP), BF16), V((ROWS, GROUP), BF16), V((2, ROWS, 256), BF16),
            V((2, ROWS, 256), BF16), V((8, ROWS), F32), V((2, 8, ROWS), F32),
            V((2, ROWS, GROUP), BF16), V((2, ROWS, GROUP), BF16),
            V((128, 256), BF16), V((256, 256), BF16), V((256, 256), BF16), V((256, 256), BF16),
            V((ROWS, 3 * ROWS), F32),
            V((HEADS, ROWS, 128), F32), V((HEADS, ROWS, 128), F32), V((HEADS, ROWS, 128), F32),
            V((HEADS, 2, ROWS, ROWS), BF16), V((2, ROWS, 256), BF16), V((2, ROWS, 256), BF16),
            dma((5,)), dma, dma((NZ,)), dma, dma((NZ,)), pltpu.SemaphoreType.REGULAR((NZ,)),
            dma((4,)), dma((2,)), dma, dma((2, 2)), dma, dma((2, 2)), dma((2,)), dma((2,)), dma((3,)),
        ],
        compiler_params=pltpu.CompilerParams(collective_id=0, has_side_effects=True),
    )(
        tokens, dest.reshape(1, ROWS), segment_ids.reshape(1, ROWS), gain.reshape(1, WIDTH),
        jnp.transpose(w_qkv, (1, 0, 2)), w_out,
    )


def solution(mesh):
    in_specs = (P("seq", None), P("seq"), P("seq"), P(), P(None, None, "head"), P("head", None))
    return jax.shard_map(
        shards, mesh=mesh, in_specs=in_specs, out_specs=P("seq", "head"), check_vma=False
    )
```

```python
import functools
import math

import jax
import jax.numpy as jnp
from jax import lax
from jax.experimental import pallas as pl
from jax.experimental.pallas import tpu as pltpu
from jax.sharding import PartitionSpec as P

MESH = pl.DeviceIdType.MESH
F32 = jnp.float32
BF16 = jnp.bfloat16
NX, NY, NZ = 4, 4, 8
NXY = NX * NY
SHARDS = NXY * NZ
ROWS = 256
WIDTH = 2048
DH = 128
GROUP = 512
HEADS = 4
CHUNKS = WIDTH // 128
SCORE = DH ** (-0.5) * math.log2(math.e)
WAVES = ((0,), (1, 7), (2, 6), (3, 5, 4))
ORDER = tuple(oz for wave in WAVES for oz in wave)
EARLY = 4


def iota(shape, dim):
    return lax.broadcasted_iota(jnp.int32, shape, dim)


def mm(a, b):
    return jnp.dot(a, b, preferred_element_type=F32)


def mm_nt(a, b):
    return lax.dot_general(a, b, (((1,), (1,)), ((), ())), preferred_element_type=F32)


def layer(
    tok_hbm, dest_hbm, seg_hbm, gain_hbm, wqkv_hbm, wout_hbm, out_ref,
    dest_ref, seg_ref, gain_ref, tok, wqkv, wo_own, wo_sib, stage, send, recv, recv_sib, xs,
    posa_src, posa, posb_src, posb, place, pool,
    k_own, v_own, q_raw, q_own, ids_src, ids_halo, k_halo, v_halo,
    crs_src, crs, line_up, far, bias, top, tot, acc, prob, at_own, at_sib,
    load_sem, row_send, row_recv, sib_send, sib_recv, go,
    pos_sem, ids_sem, k_send, k_recv, v_send, v_recv, crs_sem, wo_sem, at_sem,
):
    me = lax.axis_index("seq")
    core = lax.axis_index("head")
    other = 1 - core
    xy, z = me // NZ, me % NZ
    y, x = xy // NX, xy % NX
    left, right = (me + SHARDS - 1) % SHARDS, (me + 1) % SHARDS

    def remote(src, dst, send_sem, recv_sem, seq, head):
        return pltpu.make_async_remote_copy(
            src_ref=src, dst_ref=dst, send_sem=send_sem, recv_sem=recv_sem,
            device_id=(seq, head), device_id_type=MESH,
        )

    def drain(ref, sem):
        pltpu.make_async_copy(ref, ref, sem).wait()

    small = [
        pltpu.make_async_copy(src, dst, load_sem.at[5 + i])
        for i, (src, dst) in enumerate(
            ((dest_hbm, dest_ref), (seg_hbm, seg_ref), (gain_hbm, gain_ref))
        )
    ]
    for load in small:
        load.start()
    load_tok = pltpu.make_async_copy(tok_hbm, tok, load_sem.at[0])
    load_tok.start()
    load_w = [
        pltpu.make_async_copy(wqkv_hbm.at[part], wqkv.at[part], load_sem.at[1 + part])
        for part in range(3)
    ]
    for part in (1, 2, 0):
        load_w[part].start()
    load_wo = pltpu.make_async_copy(
        wout_hbm.at[:, pl.ds(pl.multiple_of(core * 1024, 1024), 1024)], wo_own, load_sem.at[4]
    )
    load_wo.start()

    barrier = pltpu.get_barrier_semaphore()
    for o in range(1, NZ):
        pl.semaphore_signal(
            barrier, inc=1, device_id=(xy * NZ + (z + o) % NZ, core), device_id_type=MESH
        )

    def greet(o, carry):
        pl.semaphore_signal(
            barrier, inc=1, device_id=(((xy + o) % NXY) * NZ + z, core), device_id_type=MESH
        )
        return carry

    lax.fori_loop(1, NXY, greet, 0)
    pl.semaphore_signal(barrier, inc=1, device_id=(me, other), device_id_type=MESH)

    for load in small:
        load.wait()
    dest = dest_ref[...]
    shard = jnp.right_shift(dest, 8).astype(F32)
    slot = jnp.bitwise_and(dest, 255).astype(F32)
    by_lane = jnp.broadcast_to(shard, (ROWS, ROWS))
    by_row = by_lane.T
    earlier = (by_lane == by_row) & (iota((ROWS, ROWS), 0) < iota((ROWS, ROWS), 1))
    rank = jnp.sum(jnp.where(earlier, 1.0, 0.0), axis=0, keepdims=True)
    hit = iota((SHARDS, ROWS), 0).astype(F32) == shard
    mine = hit & (rank == core.astype(F32))
    pick = jnp.where(mine, 1.0, 0.0).astype(BF16)
    pair = iota((8, ROWS), 0).astype(F32) == rank
    slots = jnp.where(pair, slot, 0.0).astype(BF16)
    posa_src[...] = mm_nt(slots, jnp.where(hit, 1.0, 0.0).astype(BF16))[0:2, :]
    load_tok.wait()
    gain = gain_ref[...]
    rows = mm(pick, tok[...])
    scale = lax.rsqrt(jnp.sum(rows * rows, axis=-1, keepdims=True) * (1.0 / WIDTH) + 1e-05)
    for j in range(CHUNKS):
        cols = slice(j * 128, (j + 1) * 128)
        stage[pl.ds(j, SHARDS, stride=CHUNKS), :] = rows[:, cols] * scale * gain[:, cols]
    send[...] = stage[...].reshape(SHARDS, CHUNKS, 128).astype(BF16)

    line = iota((256, 256), 0)
    head_at, unit = line // 64, line % 16
    level_at = (line % 64) // 16
    origin = jnp.where(
        level_at == 0, head_at * 16 + unit,
        jnp.where(
            level_at == 1, 64 + (unit // 8) * 32 + head_at * 8 + unit % 8,
            jnp.where(
                level_at == 2, 128 + (unit // 4) * 16 + head_at * 4 + unit % 4,
                192 + (unit // 2) * 8 + head_at * 2 + unit % 2,
            ),
        ),
    )
    line_up[...] = jnp.where(iota((256, 256), 1) == origin, 1.0, 0.0).astype(BF16)

    pl.semaphore_wait(barrier, NZ - 1 + NXY)
    for o in range(1, NZ):
        pl.semaphore_signal(
            go.at[NZ - o], inc=1, device_id=(xy * NZ + (z + o) % NZ, core), device_id_type=MESH
        )

    posa[z] = posa_src[...]
    for o in range(1, NZ):
        remote(
            posa_src, posa.at[z], pos_sem.at[0], pos_sem.at[1], xy * NZ + (z + o) % NZ, core,
        ).start()

    def send_rows(first, wave):
        def body(i, carry):
            at = ((y + i // NX) % NY) * NX + (x + i % NX) % NX
            for oz in wave:
                group = ORDER.index(oz)
                peer = at * NZ + (z + oz) % NZ
                remote(
                    send.at[peer], recv.at[group * NXY + xy], row_send, row_recv.at[group],
                    peer, core,
                ).start()
            return carry

        lax.fori_loop(first, NXY, body, 0)

    pltpu.make_async_copy(send.at[me], recv.at[xy], row_recv.at[0]).start()
    send_rows(1, WAVES[0])
    for wave in WAVES[1:]:
        for oz in wave:
            pl.semaphore_wait(go.at[oz], 1)
        send_rows(0, wave)
    drain(posa.at[pl.ds(0, NZ - 1)], pos_sem.at[1])
    for oz in range(NZ):
        for k in range(2):
            posb_src[k * NZ + oz:k * NZ + oz + 1, :] = posa[oz, k:k + 1, :]
    posb[pl.ds(pl.multiple_of(xy * 16, 16), 16), :] = posb_src[...]

    def send_pos(o, carry):
        remote(
            posb_src, posb.at[pl.ds(pl.multiple_of(xy * 16, 16), 16)], pos_sem.at[2],
            pos_sem.at[3], ((xy + o) % NXY) * NZ + z, core,
        ).start()
        return carry

    lax.fori_loop(1, NXY, send_pos, 0)

    def unpack(group, landed, line):
        part = pl.ds(group * NXY * CHUNKS, NXY * CHUNKS)
        stage[part, :] = (
            landed[group * NXY:(group + 1) * NXY].astype(F32).reshape(NXY * CHUNKS, 128)
        )
        for j in range(CHUNKS):
            xs[line:line + NXY, j * 128:(j + 1) * 128] = (
                stage[pl.ds(group * NXY * CHUNKS + j, NXY, stride=CHUNKS), :].astype(BF16)
            )

    def collect(first):
        base = (first // EARLY) * 128
        for group in range(first, first + EARLY):
            block = pl.ds(group * NXY, NXY)
            drain(recv.at[block], row_recv.at[group])
            remote(
                recv.at[block], recv_sib.at[block], sib_send, sib_recv.at[group], me, other
            ).start()
            unpack(group, recv, base + (group - first) * NXY)
        for group in range(first, first + EARLY):
            drain(recv_sib.at[pl.ds(group * NXY, NXY)], sib_recv.at[group])
            unpack(group, recv_sib, base + 64 + (group - first) * NXY)

    def project(part, own, half):
        lines = slice(half * 128, (half + 1) * 128)
        own[lines, :] = mm(xs[lines, :], wqkv[part]).astype(BF16)

    def send_halo(own, halo, half, send_sem, recv_sem):
        lines = pl.ds(half * 128, 128)
        for side, peer in ((1, left), (0, right)):
            remote(
                own.at[lines], halo.at[side, lines], send_sem, recv_sem.at[side, half], peer, core
            ).start()

    collect(0)
    load_w[1].wait()
    load_w[2].wait()
    project(1, k_own, 0)
    send_halo(k_own, k_halo, 0, k_send, k_recv)
    project(2, v_own, 0)
    send_halo(v_own, v_halo, 0, v_send, v_recv)

    collect(EARLY)
    project(1, k_own, 1)
    send_halo(k_own, k_halo, 1, k_send, k_recv)
    project(2, v_own, 1)

    drain(posb.at[pl.ds(0, 240)], pos_sem.at[3])
    pieces = []
    for first in (0, EARLY):
        for who in (core, other):
            for oz in ORDER[first:first + EARLY]:
                pieces.append(posb[pl.ds(who * NZ + (z + NZ - oz) % NZ, NXY, stride=16), :])
    table = jnp.concatenate(pieces, axis=0).astype(BF16)
    my_lane = jnp.where(iota((8, 128), 1) == me, 1.0, 0.0).astype(BF16)
    pos_row = mm_nt(my_lane, table)[0:1, :]
    where_to = jnp.where(iota((ROWS, ROWS), 0).astype(F32) == pos_row, 1.0, 0.0).astype(BF16)
    place[...] = where_to
    seg = seg_ref[...].astype(F32)
    ids_src[...] = mm(jnp.broadcast_to(seg, (8, ROWS)).astype(BF16), where_to)
    for side, peer in ((1, left), (0, right)):
        remote(ids_src, ids_halo.at[side], ids_sem.at[0], ids_sem.at[1], peer, core).start()

    place_int = pos_row.astype(jnp.int32)
    line = iota((128, ROWS), 0)
    spread = jnp.broadcast_to(place_int, (128, ROWS))
    weights = jnp.zeros((128, ROWS), F32)
    start = 0
    for level in range(4):
        count = 16 >> level
        inside = (line >= start) & (line < start + HEADS * count)
        same = jnp.right_shift(spread, 4 + level) == (line - start) % count
        weights = jnp.where(inside & same, 1.0 / (16 << level), weights)
        start += HEADS * count
    pool[...] = weights.astype(BF16)

    own_col = jnp.broadcast_to(seg, (ROWS, ROWS)).T
    bias[:, 0:ROWS] = jnp.where(own_col == ids_src[0:1, :], 0.0, -jnp.inf)

    line = iota((128, 128), 0)
    head_of = jnp.where(
        line < 64, line // 16,
        jnp.where(line < 96, (line - 64) // 8, jnp.where(line < 112, (line - 96) // 4, (line - 112) // 2)),
    )
    for which, own in ((0, k_own), (1, v_own)):
        picked = jnp.zeros((128, 128), F32)
        for half in range(2):
            means = mm(pool[...], own[:, half * 256:(half + 1) * 256])
            for sub in range(2):
                picked = jnp.where(
                    head_of == half * 2 + sub, means[:, sub * 128:(sub + 1) * 128], picked
                )
        crs_src[:, which * 128:(which + 1) * 128] = picked.astype(BF16)
    start = 0
    for level in range(4):
        size = 1 << level
        lines = 64 >> level
        group = me // size
        partner = group + 1 - 2 * (group % 2)
        for i in range(size):
            remote(
                crs_src.at[pl.ds(start, lines)],
                crs.at[pl.ds(pl.multiple_of(64 * level + (me % size) * lines, 8), lines)],
                crs_sem.at[0], crs_sem.at[1], partner * size + i, core,
            ).start()
        start += lines
    send_halo(v_own, v_halo, 1, v_send, v_recv)
    remote(
        wout_hbm.at[:, pl.ds(pl.multiple_of(other * 1024, 1024), 1024)], wo_sib,
        wo_sem.at[0], wo_sem.at[1], me, other,
    ).start()

    load_w[0].wait()
    for half in range(2):
        cols = slice(half * 256, (half + 1) * 256)
        q_raw[half] = mm(xs[...], wqkv[0, :, cols]).astype(BF16)
    for half in range(2):
        q_own[half] = mm(place[...], q_raw[half]).astype(BF16)

    def head(ref, h):
        return ref[:, h * 128:(h + 1) * 128]

    def fine(h, keys, mask):
        return mm_nt(q_own[h // 2, :, (h % 2) * 128:(h % 2 + 1) * 128], keys) * SCORE + mask

    for h in range(HEADS):
        score = fine(h, head(k_own, h), bias[:, 0:ROWS])
        best = jnp.max(score, axis=-1, keepdims=True)
        weight = jnp.exp2(score - best)
        tot[h] = jnp.broadcast_to(jnp.sum(weight, axis=-1, keepdims=True), (ROWS, 128))
        top[h] = jnp.broadcast_to(best, (ROWS, 128))
        acc[h] = mm(weight.astype(BF16), head(v_own, h))

    drain(ids_halo, ids_sem.at[1])
    own_col = jnp.broadcast_to(seg, (ROWS, ROWS)).T
    edge = ((me > 0), (me < SHARDS - 1))
    for side in range(2):
        same = own_col == ids_halo[side][0:1, :]
        bias[:, (side + 1) * ROWS:(side + 2) * ROWS] = jnp.where(same & edge[side], 0.0, -jnp.inf)

    for half in range(2):
        for side in range(2):
            drain(k_halo.at[side, pl.ds(half * 128, 128)], k_recv.at[side, half])
    drain(crs, crs_sem.at[1])
    far[...] = mm(line_up[...], crs[...]).astype(BF16)
    lift = (iota((8, 64), 1) // 16 + 4).astype(F32)[0:1, :]

    for h in range(HEADS):
        scores = [
            fine(h, head(k_halo.at[side], h), bias[:, (side + 1) * ROWS:(side + 2) * ROWS])
            for side in range(2)
        ]
        scores.append(fine(h, far[h * 64:(h + 1) * 64, 0:128], lift))
        old = top[h][:, 0:1]
        best = old
        for score in scores:
            best = jnp.maximum(best, jnp.max(score, axis=-1, keepdims=True))
        fade = jnp.exp2(old - best)
        weight = jnp.exp2(scores[2] - best)
        total = tot[h] * fade + jnp.sum(weight, axis=-1, keepdims=True)
        acc[h] = acc[h] * fade + mm(weight.astype(BF16), far[h * 64:(h + 1) * 64, 128:256])
        for side in range(2):
            weight = jnp.exp2(scores[side] - best)
            total = total + jnp.sum(weight, axis=-1, keepdims=True)
            prob[h, side] = weight.astype(BF16)
        tot[h] = total

    load_wo.wait()
    for half in range(2):
        for side in range(2):
            drain(v_halo.at[side, pl.ds(half * 128, 128)], v_recv.at[side, half])
    for half in range(2):
        for h in (half * 2, half * 2 + 1):
            total = acc[h]
            for side in range(2):
                total = total + mm(prob[h, side], head(v_halo.at[side], h))
            at_own[half, :, (h % 2) * 128:(h % 2 + 1) * 128] = (total / tot[h]).astype(BF16)
        remote(
            at_own.at[half], at_sib.at[half], at_sem.at[0], at_sem.at[1 + half], me, other
        ).start()

    drain(wo_sib, wo_sem.at[1])
    for half in range(2):
        drain(at_sib.at[half], at_sem.at[1 + half])
    for part in range(4):
        cols = slice(part * 256, (part + 1) * 256)
        total = jnp.zeros((ROWS, 256), F32)
        for half in range(2):
            lines = slice(half * 256, (half + 1) * 256)
            total = total + mm(at_own[half], wo_own[lines, cols])
            total = total + mm(at_sib[half], wo_sib[lines, cols])
        out_ref[:, cols] = total.astype(BF16)

    drain(send.at[pl.ds(0, SHARDS - 1)], row_send)
    drain(posa.at[pl.ds(0, NZ - 1)], pos_sem.at[0])
    drain(posb.at[pl.ds(0, 240)], pos_sem.at[2])
    drain(ids_halo, ids_sem.at[0])
    drain(recv, sib_send)
    drain(k_halo, k_send)
    drain(v_halo, v_send)
    drain(crs, crs_sem.at[0])
    drain(wo_sib, wo_sem.at[0])
    drain(at_own, at_sem.at[0])


def shards(tokens, dest, segment_ids, gain, w_qkv, w_out):
    vmem = pl.BlockSpec(memory_space=pltpu.VMEM)
    hbm = pl.BlockSpec(memory_space=pltpu.HBM)
    dma = pltpu.SemaphoreType.DMA
    keep = lambda a: pltpu.with_memory_space_constraint(a, pltpu.HBM)
    V = pltpu.VMEM
    return pl.pallas_call(
        layer,
        out_shape=jax.ShapeDtypeStruct((ROWS, 1024), BF16),
        in_specs=[hbm] * 6,
        out_specs=vmem,
        scratch_shapes=[
            V((1, ROWS), jnp.int32), V((1, ROWS), jnp.int32), V((1, WIDTH), F32),
            V((ROWS, WIDTH), BF16), V((3, WIDTH, GROUP), BF16), V((GROUP, 1024), BF16),
            V((GROUP, 1024), BF16), V((SHARDS * CHUNKS, 128), F32), V((SHARDS, CHUNKS, 128), BF16),
            V((SHARDS, CHUNKS, 128), BF16), V((SHARDS, CHUNKS, 128), BF16), V((ROWS, WIDTH), BF16),
            V((2, 128), F32), V((NZ, 2, 128), F32), V((16, 128), F32), V((256, 128), F32),
            V((ROWS, ROWS), BF16), V((128, ROWS), BF16),
            V((ROWS, GROUP), BF16), V((ROWS, GROUP), BF16), V((2, ROWS, 256), BF16),
            V((2, ROWS, 256), BF16), V((8, ROWS), F32), V((2, 8, ROWS), F32),
            V((2, ROWS, GROUP), BF16), V((2, ROWS, GROUP), BF16),
            V((128, 256), BF16), V((256, 256), BF16), V((256, 256), BF16), V((256, 256), BF16),
            V((ROWS, 3 * ROWS), F32),
            V((HEADS, ROWS, 128), F32), V((HEADS, ROWS, 128), F32), V((HEADS, ROWS, 128), F32),
            V((HEADS, 2, ROWS, ROWS), BF16), V((2, ROWS, 256), BF16), V((2, ROWS, 256), BF16),
            dma((8,)), dma, dma((NZ,)), dma, dma((NZ,)), pltpu.SemaphoreType.REGULAR((NZ,)),
            dma((4,)), dma((2,)), dma, dma((2, 2)), dma, dma((2, 2)), dma((2,)), dma((2,)), dma((3,)),
        ],
        compiler_params=pltpu.CompilerParams(collective_id=0, has_side_effects=True, vmem_limit_bytes=40 * 2**20),
    )(
        keep(tokens), keep(dest.reshape(1, ROWS)), keep(segment_ids.reshape(1, ROWS)),
        keep(gain.reshape(1, WIDTH)),
        keep(jnp.transpose(w_qkv, (1, 0, 2))), keep(w_out),
    )


def solution(mesh):
    in_specs = (P("seq", None), P("seq"), P("seq"), P(), P(None, None, "head"), P("head", None))
    return jax.shard_map(
        shards, mesh=mesh, in_specs=in_specs, out_specs=P("seq", "head"), check_vma=False
    )
```

```python
import functools
import math

import jax
import jax.numpy as jnp
from jax import lax
from jax.experimental import pallas as pl
from jax.experimental.pallas import tpu as pltpu
from jax.sharding import PartitionSpec as P

MESH = pl.DeviceIdType.MESH
F32 = jnp.float32
BF16 = jnp.bfloat16
NX, NY, NZ = 4, 4, 8
NXY = NX * NY
SHARDS = NXY * NZ
ROWS = 256
WIDTH = 2048
DH = 128
GROUP = 512
HEADS = 4
CHUNKS = WIDTH // 128
SCORE = DH ** (-0.5) * math.log2(math.e)
WAVES = ((0,), (1, 7), (2, 6), (3, 5, 4))
ORDER = tuple(oz for wave in WAVES for oz in wave)
PARTS = (0, 3, 5, 8)


def iota(shape, dim):
    return lax.broadcasted_iota(jnp.int32, shape, dim)


def mm(a, b):
    return jnp.dot(a, b, preferred_element_type=F32)


def mm_nt(a, b):
    return lax.dot_general(a, b, (((1,), (1,)), ((), ())), preferred_element_type=F32)


def layer(
    tok_hbm, dest_hbm, seg_hbm, gain_hbm, wqkv_hbm, wout_hbm, out_ref,
    dest_ref, seg_ref, gain_ref, tok, wqkv, wo_own, wo_sib, stage, send, recv, recv_sib, xs,
    posa_src, posa, posb_src, posb, place, pool,
    k_own, v_own, q_raw, q_own, ids_src, ids_halo, k_halo, v_halo,
    crs_src, crs, line_up, far, bias, top, tot, acc, prob, at_own, at_sib,
    load_sem, row_send, row_recv, sib_send, sib_recv, go,
    pos_sem, ids_sem, k_send, k_recv, v_send, v_recv, crs_sem, wo_sem, at_sem,
):
    me = lax.axis_index("seq")
    core = lax.axis_index("head")
    other = 1 - core
    xy, z = me // NZ, me % NZ
    y, x = xy // NX, xy % NX
    left, right = (me + SHARDS - 1) % SHARDS, (me + 1) % SHARDS

    def remote(src, dst, send_sem, recv_sem, seq, head):
        return pltpu.make_async_remote_copy(
            src_ref=src, dst_ref=dst, send_sem=send_sem, recv_sem=recv_sem,
            device_id=(seq, head), device_id_type=MESH,
        )

    def drain(ref, sem):
        pltpu.make_async_copy(ref, ref, sem).wait()

    small = [
        pltpu.make_async_copy(src, dst, load_sem.at[5 + i])
        for i, (src, dst) in enumerate(
            ((dest_hbm, dest_ref), (seg_hbm, seg_ref), (gain_hbm, gain_ref))
        )
    ]
    for load in small:
        load.start()
    load_tok = pltpu.make_async_copy(tok_hbm, tok, load_sem.at[0])
    load_tok.start()
    load_w = [
        pltpu.make_async_copy(wqkv_hbm.at[part], wqkv.at[part], load_sem.at[1 + part])
        for part in range(3)
    ]
    for part in (1, 2, 0):
        load_w[part].start()
    load_wo = pltpu.make_async_copy(
        wout_hbm.at[:, pl.ds(pl.multiple_of(core * 1024, 1024), 1024)], wo_own, load_sem.at[4]
    )
    load_wo.start()

    barrier = pltpu.get_barrier_semaphore()
    for o in range(1, NZ):
        pl.semaphore_signal(
            barrier, inc=1, device_id=(xy * NZ + (z + o) % NZ, core), device_id_type=MESH
        )

    def greet(o, carry):
        pl.semaphore_signal(
            barrier, inc=1, device_id=(((xy + o) % NXY) * NZ + z, core), device_id_type=MESH
        )
        return carry

    lax.fori_loop(1, NXY, greet, 0)
    pl.semaphore_signal(barrier, inc=1, device_id=(me, other), device_id_type=MESH)

    for load in small:
        load.wait()
    dest = dest_ref[...]
    shard = jnp.right_shift(dest, 8).astype(F32)
    slot = jnp.bitwise_and(dest, 255).astype(F32)
    by_lane = jnp.broadcast_to(shard, (ROWS, ROWS))
    by_row = by_lane.T
    earlier = (by_lane == by_row) & (iota((ROWS, ROWS), 0) < iota((ROWS, ROWS), 1))
    rank = jnp.sum(jnp.where(earlier, 1.0, 0.0), axis=0, keepdims=True)
    hit = iota((SHARDS, ROWS), 0).astype(F32) == shard
    mine = hit & (rank == core.astype(F32))
    pick = jnp.where(mine, 1.0, 0.0).astype(BF16)
    pair = iota((8, ROWS), 0).astype(F32) == rank
    slots = jnp.where(pair, slot, 0.0).astype(BF16)
    posa_src[...] = mm_nt(slots, jnp.where(hit, 1.0, 0.0).astype(BF16))[0:2, :]
    load_tok.wait()
    gain = gain_ref[...]
    rows = mm(pick, tok[...])
    scale = lax.rsqrt(jnp.sum(rows * rows, axis=-1, keepdims=True) * (1.0 / WIDTH) + 1e-05)
    for j in range(CHUNKS):
        cols = slice(j * 128, (j + 1) * 128)
        stage[pl.ds(j, SHARDS, stride=CHUNKS), :] = rows[:, cols] * scale * gain[:, cols]
    send[...] = stage[...].reshape(SHARDS, CHUNKS, 128).astype(BF16)

    line = iota((256, 256), 0)
    head_at, unit = line // 64, line % 16
    level_at = (line % 64) // 16
    origin = jnp.where(
        level_at == 0, head_at * 16 + unit,
        jnp.where(
            level_at == 1, 64 + (unit // 8) * 32 + head_at * 8 + unit % 8,
            jnp.where(
                level_at == 2, 128 + (unit // 4) * 16 + head_at * 4 + unit % 4,
                192 + (unit // 2) * 8 + head_at * 2 + unit % 2,
            ),
        ),
    )
    line_up[...] = jnp.where(iota((256, 256), 1) == origin, 1.0, 0.0).astype(BF16)

    pl.semaphore_wait(barrier, NZ - 1 + NXY)
    for o in range(1, NZ):
        pl.semaphore_signal(
            go.at[NZ - o], inc=1, device_id=(xy * NZ + (z + o) % NZ, core), device_id_type=MESH
        )

    posa[z] = posa_src[...]
    for o in range(1, NZ):
        remote(
            posa_src, posa.at[z], pos_sem.at[0], pos_sem.at[1], xy * NZ + (z + o) % NZ, core,
        ).start()

    def send_rows(first, wave):
        def body(i, carry):
            at = ((y + i // NX) % NY) * NX + (x + i % NX) % NX
            for oz in wave:
                group = ORDER.index(oz)
                peer = at * NZ + (z + oz) % NZ
                remote(
                    send.at[peer], recv.at[group * NXY + xy], row_send, row_recv.at[group],
                    peer, core,
                ).start()
            return carry

        lax.fori_loop(first, NXY, body, 0)

    pltpu.make_async_copy(send.at[me], recv.at[xy], row_recv.at[0]).start()
    send_rows(1, WAVES[0])
    for wave in WAVES[1:]:
        for oz in wave:
            pl.semaphore_wait(go.at[oz], 1)
        send_rows(0, wave)
    drain(posa.at[pl.ds(0, NZ - 1)], pos_sem.at[1])
    for oz in range(NZ):
        for k in range(2):
            posb_src[k * NZ + oz:k * NZ + oz + 1, :] = posa[oz, k:k + 1, :]
    posb[pl.ds(pl.multiple_of(xy * 16, 16), 16), :] = posb_src[...]

    def send_pos(o, carry):
        remote(
            posb_src, posb.at[pl.ds(pl.multiple_of(xy * 16, 16), 16)], pos_sem.at[2],
            pos_sem.at[3], ((xy + o) % NXY) * NZ + z, core,
        ).start()
        return carry

    lax.fori_loop(1, NXY, send_pos, 0)

    def unpack(group, landed, line):
        part = pl.ds(group * NXY * CHUNKS, NXY * CHUNKS)
        stage[part, :] = (
            landed[group * NXY:(group + 1) * NXY].astype(F32).reshape(NXY * CHUNKS, 128)
        )
        for j in range(CHUNKS):
            xs[line:line + NXY, j * 128:(j + 1) * 128] = (
                stage[pl.ds(group * NXY * CHUNKS + j, NXY, stride=CHUNKS), :].astype(BF16)
            )

    def collect(part):
        first, last = PARTS[part], PARTS[part + 1]
        line = 2 * NXY * first
        for group in range(first, last):
            block = pl.ds(group * NXY, NXY)
            drain(recv.at[block], row_recv.at[group])
            remote(
                recv.at[block], recv_sib.at[block], sib_send, sib_recv.at[group], me, other
            ).start()
            unpack(group, recv, line)
            line += NXY
        for group in range(first, last):
            drain(recv_sib.at[pl.ds(group * NXY, NXY)], sib_recv.at[group])
            unpack(group, recv_sib, line)
            line += NXY

    def span(number):
        return pl.ds(2 * NXY * PARTS[number], 2 * NXY * (PARTS[number + 1] - PARTS[number]))

    def project(part, own, number):
        lines = span(number)
        own[lines, :] = mm(xs[lines, :], wqkv[part]).astype(BF16)

    def send_halo(own, halo, number, send_sem, recv_sem):
        lines = span(number)
        for side, peer in ((1, left), (0, right)):
            remote(
                own.at[lines], halo.at[side, lines], send_sem, recv_sem.at[side, number], peer, core
            ).start()

    last = len(PARTS) - 2
    for number in range(last + 1):
        collect(number)
        if number == 0:
            load_w[1].wait()
            load_w[2].wait()
        project(1, k_own, number)
        send_halo(k_own, k_halo, number, k_send, k_recv)
        project(2, v_own, number)
        if number < last:
            send_halo(v_own, v_halo, number, v_send, v_recv)

    drain(posb.at[pl.ds(0, 240)], pos_sem.at[3])
    pieces = []
    for number in range(last + 1):
        for who in (core, other):
            for oz in ORDER[PARTS[number]:PARTS[number + 1]]:
                pieces.append(posb[pl.ds(who * NZ + (z + NZ - oz) % NZ, NXY, stride=16), :])
    table = jnp.concatenate(pieces, axis=0).astype(BF16)
    my_lane = jnp.where(iota((8, 128), 1) == me, 1.0, 0.0).astype(BF16)
    pos_row = mm_nt(my_lane, table)[0:1, :]
    where_to = jnp.where(iota((ROWS, ROWS), 0).astype(F32) == pos_row, 1.0, 0.0).astype(BF16)
    place[...] = where_to
    seg = seg_ref[...].astype(F32)
    ids_src[...] = mm(jnp.broadcast_to(seg, (8, ROWS)).astype(BF16), where_to)
    for side, peer in ((1, left), (0, right)):
        remote(ids_src, ids_halo.at[side], ids_sem.at[0], ids_sem.at[1], peer, core).start()

    place_int = pos_row.astype(jnp.int32)
    line = iota((128, ROWS), 0)
    spread = jnp.broadcast_to(place_int, (128, ROWS))
    weights = jnp.zeros((128, ROWS), F32)
    start = 0
    for level in range(4):
        count = 16 >> level
        inside = (line >= start) & (line < start + HEADS * count)
        same = jnp.right_shift(spread, 4 + level) == (line - start) % count
        weights = jnp.where(inside & same, 1.0 / (16 << level), weights)
        start += HEADS * count
    pool[...] = weights.astype(BF16)

    own_col = jnp.broadcast_to(seg, (ROWS, ROWS)).T
    bias[:, 0:ROWS] = jnp.where(own_col == ids_src[0:1, :], 0.0, -jnp.inf)

    line = iota((128, 128), 0)
    head_of = jnp.where(
        line < 64, line // 16,
        jnp.where(line < 96, (line - 64) // 8, jnp.where(line < 112, (line - 96) // 4, (line - 112) // 2)),
    )
    for which, own in ((0, k_own), (1, v_own)):
        picked = jnp.zeros((128, 128), F32)
        for half in range(2):
            means = mm(pool[...], own[:, half * 256:(half + 1) * 256])
            for sub in range(2):
                picked = jnp.where(
                    head_of == half * 2 + sub, means[:, sub * 128:(sub + 1) * 128], picked
                )
        crs_src[:, which * 128:(which + 1) * 128] = picked.astype(BF16)
    start = 0
    for level in range(4):
        size = 1 << level
        lines = 64 >> level
        group = me // size
        partner = group + 1 - 2 * (group % 2)
        for i in range(size):
            remote(
                crs_src.at[pl.ds(start, lines)],
                crs.at[pl.ds(pl.multiple_of(64 * level + (me % size) * lines, 8), lines)],
                crs_sem.at[0], crs_sem.at[1], partner * size + i, core,
            ).start()
        start += lines
    send_halo(v_own, v_halo, last, v_send, v_recv)
    remote(
        wout_hbm.at[:, pl.ds(pl.multiple_of(other * 1024, 1024), 1024)], wo_sib,
        wo_sem.at[0], wo_sem.at[1], me, other,
    ).start()

    load_w[0].wait()
    for half in range(2):
        cols = slice(half * 256, (half + 1) * 256)
        q_raw[half] = mm(xs[...], wqkv[0, :, cols]).astype(BF16)
    for half in range(2):
        q_own[half] = mm(place[...], q_raw[half]).astype(BF16)

    def head(ref, h):
        return ref[:, h * 128:(h + 1) * 128]

    def fine(h, keys, mask):
        return mm_nt(q_own[h // 2, :, (h % 2) * 128:(h % 2 + 1) * 128], keys) * SCORE + mask

    for h in range(HEADS):
        score = fine(h, head(k_own, h), bias[:, 0:ROWS])
        best = jnp.max(score, axis=-1, keepdims=True)
        weight = jnp.exp2(score - best)
        tot[h] = jnp.broadcast_to(jnp.sum(weight, axis=-1, keepdims=True), (ROWS, 128))
        top[h] = jnp.broadcast_to(best, (ROWS, 128))
        acc[h] = mm(weight.astype(BF16), head(v_own, h))

    drain(ids_halo, ids_sem.at[1])
    own_col = jnp.broadcast_to(seg, (ROWS, ROWS)).T
    edge = ((me > 0), (me < SHARDS - 1))
    for side in range(2):
        same = own_col == ids_halo[side][0:1, :]
        bias[:, (side + 1) * ROWS:(side + 2) * ROWS] = jnp.where(same & edge[side], 0.0, -jnp.inf)

    for number in range(last + 1):
        for side in range(2):
            drain(k_halo.at[side, span(number)], k_recv.at[side, number])
    drain(crs, crs_sem.at[1])
    far[...] = mm(line_up[...], crs[...]).astype(BF16)
    lift = (iota((8, 64), 1) // 16 + 4).astype(F32)[0:1, :]

    for h in range(HEADS):
        scores = [
            fine(h, head(k_halo.at[side], h), bias[:, (side + 1) * ROWS:(side + 2) * ROWS])
            for side in range(2)
        ]
        scores.append(fine(h, far[h * 64:(h + 1) * 64, 0:128], lift))
        old = top[h][:, 0:1]
        best = old
        for score in scores:
            best = jnp.maximum(best, jnp.max(score, axis=-1, keepdims=True))
        fade = jnp.exp2(old - best)
        weight = jnp.exp2(scores[2] - best)
        total = tot[h] * fade + jnp.sum(weight, axis=-1, keepdims=True)
        acc[h] = acc[h] * fade + mm(weight.astype(BF16), far[h * 64:(h + 1) * 64, 128:256])
        for side in range(2):
            weight = jnp.exp2(scores[side] - best)
            total = total + jnp.sum(weight, axis=-1, keepdims=True)
            prob[h, side] = weight.astype(BF16)
        tot[h] = total

    load_wo.wait()
    for number in range(last + 1):
        for side in range(2):
            drain(v_halo.at[side, span(number)], v_recv.at[side, number])
    for half in range(2):
        for h in (half * 2, half * 2 + 1):
            total = acc[h]
            for side in range(2):
                total = total + mm(prob[h, side], head(v_halo.at[side], h))
            at_own[half, :, (h % 2) * 128:(h % 2 + 1) * 128] = (total / tot[h]).astype(BF16)
        remote(
            at_own.at[half], at_sib.at[half], at_sem.at[0], at_sem.at[1 + half], me, other
        ).start()

    drain(wo_sib, wo_sem.at[1])
    for half in range(2):
        drain(at_sib.at[half], at_sem.at[1 + half])
    for part in range(4):
        cols = slice(part * 256, (part + 1) * 256)
        total = jnp.zeros((ROWS, 256), F32)
        for half in range(2):
            lines = slice(half * 256, (half + 1) * 256)
            total = total + mm(at_own[half], wo_own[lines, cols])
            total = total + mm(at_sib[half], wo_sib[lines, cols])
        out_ref[:, cols] = total.astype(BF16)

    drain(send.at[pl.ds(0, SHARDS - 1)], row_send)
    drain(posa.at[pl.ds(0, NZ - 1)], pos_sem.at[0])
    drain(posb.at[pl.ds(0, 240)], pos_sem.at[2])
    drain(ids_halo, ids_sem.at[0])
    drain(recv, sib_send)
    drain(k_halo, k_send)
    drain(v_halo, v_send)
    drain(crs, crs_sem.at[0])
    drain(wo_sib, wo_sem.at[0])
    drain(at_own, at_sem.at[0])


def shards(tokens, dest, segment_ids, gain, w_qkv, w_out):
    vmem = pl.BlockSpec(memory_space=pltpu.VMEM)
    hbm = pl.BlockSpec(memory_space=pltpu.HBM)
    dma = pltpu.SemaphoreType.DMA
    keep = lambda a: pltpu.with_memory_space_constraint(a, pltpu.HBM)
    V = pltpu.VMEM
    return pl.pallas_call(
        layer,
        out_shape=jax.ShapeDtypeStruct((ROWS, 1024), BF16),
        in_specs=[hbm] * 6,
        out_specs=vmem,
        scratch_shapes=[
            V((1, ROWS), jnp.int32), V((1, ROWS), jnp.int32), V((1, WIDTH), F32),
            V((ROWS, WIDTH), BF16), V((3, WIDTH, GROUP), BF16), V((GROUP, 1024), BF16),
            V((GROUP, 1024), BF16), V((SHARDS * CHUNKS, 128), F32), V((SHARDS, CHUNKS, 128), BF16),
            V((SHARDS, CHUNKS, 128), BF16), V((SHARDS, CHUNKS, 128), BF16), V((ROWS, WIDTH), BF16),
            V((2, 128), F32), V((NZ, 2, 128), F32), V((16, 128), F32), V((256, 128), F32),
            V((ROWS, ROWS), BF16), V((128, ROWS), BF16),
            V((ROWS, GROUP), BF16), V((ROWS, GROUP), BF16), V((2, ROWS, 256), BF16),
            V((2, ROWS, 256), BF16), V((8, ROWS), F32), V((2, 8, ROWS), F32),
            V((2, ROWS, GROUP), BF16), V((2, ROWS, GROUP), BF16),
            V((128, 256), BF16), V((256, 256), BF16), V((256, 256), BF16), V((256, 256), BF16),
            V((ROWS, 3 * ROWS), F32),
            V((HEADS, ROWS, 128), F32), V((HEADS, ROWS, 128), F32), V((HEADS, ROWS, 128), F32),
            V((HEADS, 2, ROWS, ROWS), BF16), V((2, ROWS, 256), BF16), V((2, ROWS, 256), BF16),
            dma((8,)), dma, dma((NZ,)), dma, dma((NZ,)), pltpu.SemaphoreType.REGULAR((NZ,)),
            dma((4,)), dma((2,)), dma, dma((2, 6)), dma, dma((2, 6)), dma((2,)), dma((2,)), dma((3,)),
        ],
        compiler_params=pltpu.CompilerParams(collective_id=0, has_side_effects=True, vmem_limit_bytes=40 * 2**20),
    )(
        keep(tokens), keep(dest.reshape(1, ROWS)), keep(segment_ids.reshape(1, ROWS)),
        keep(gain.reshape(1, WIDTH)),
        keep(jnp.transpose(w_qkv, (1, 0, 2))), keep(w_out),
    )


def solution(mesh):
    in_specs = (P("seq", None), P("seq"), P("seq"), P(), P(None, None, "head"), P("head", None))
    return jax.shard_map(
        shards, mesh=mesh, in_specs=in_specs, out_specs=P("seq", "head"), check_vma=False
    )
```

```python
import functools
import math

import jax
import jax.numpy as jnp
from jax import lax
from jax.experimental import pallas as pl
from jax.experimental.pallas import tpu as pltpu
from jax.sharding import PartitionSpec as P

MESH = pl.DeviceIdType.MESH
F32 = jnp.float32
BF16 = jnp.bfloat16
NX, NY, NZ = 4, 4, 8
NXY = NX * NY
SHARDS = NXY * NZ
ROWS = 256
WIDTH = 2048
DH = 128
GROUP = 512
HEADS = 4
CHUNKS = WIDTH // 128
SCORE = DH ** (-0.5) * math.log2(math.e)
WAVES = ((0,), (1, 7), (2, 6), (3, 5, 4))
ORDER = tuple(oz for wave in WAVES for oz in wave)
PARTS = (0, 3, 5, 8)


def iota(shape, dim):
    return lax.broadcasted_iota(jnp.int32, shape, dim)


def mm(a, b):
    return jnp.dot(a, b, preferred_element_type=F32)


def mm_nt(a, b):
    return lax.dot_general(a, b, (((1,), (1,)), ((), ())), preferred_element_type=F32)


def layer(
    tok_hbm, dest_hbm, seg_hbm, gain_hbm, wqkv_hbm, wout_hbm, out_ref,
    dest_ref, seg_ref, gain_ref, tok, wqkv, wo_own, wo_sib, stage, send, recv, recv_sib, xs,
    posa_src, posa, posb_src, posb, place, pool,
    k_own, v_own, q_raw, q_own, ids_src, ids_halo, k_halo, v_halo,
    crs_src, crs, line_up, far, bias, top, tot, acc, prob, at_own, at_sib, sums, far_sum,
    load_sem, row_send, row_recv, sib_send, sib_recv, go,
    pos_sem, ids_sem, k_send, k_recv, v_send, v_recv, crs_sem, wo_sem, at_sem,
):
    me = lax.axis_index("seq")
    core = lax.axis_index("head")
    other = 1 - core
    xy, z = me // NZ, me % NZ
    y, x = xy // NX, xy % NX
    left, right = (me + SHARDS - 1) % SHARDS, (me + 1) % SHARDS

    def remote(src, dst, send_sem, recv_sem, seq, head):
        return pltpu.make_async_remote_copy(
            src_ref=src, dst_ref=dst, send_sem=send_sem, recv_sem=recv_sem,
            device_id=(seq, head), device_id_type=MESH,
        )

    def drain(ref, sem):
        pltpu.make_async_copy(ref, ref, sem).wait()

    small = [
        pltpu.make_async_copy(src, dst, load_sem.at[5 + i])
        for i, (src, dst) in enumerate(
            ((dest_hbm, dest_ref), (seg_hbm, seg_ref), (gain_hbm, gain_ref))
        )
    ]
    for load in small:
        load.start()
    load_tok = pltpu.make_async_copy(tok_hbm, tok, load_sem.at[0])
    load_tok.start()
    load_w = [
        pltpu.make_async_copy(wqkv_hbm.at[part], wqkv.at[part], load_sem.at[1 + part])
        for part in range(3)
    ]
    for part in (1, 2, 0):
        load_w[part].start()
    load_wo = pltpu.make_async_copy(
        wout_hbm.at[:, pl.ds(pl.multiple_of(core * 1024, 1024), 1024)], wo_own, load_sem.at[4]
    )
    load_wo.start()

    barrier = pltpu.get_barrier_semaphore()
    for o in range(1, NZ):
        pl.semaphore_signal(
            barrier, inc=1, device_id=(xy * NZ + (z + o) % NZ, core), device_id_type=MESH
        )

    def greet(o, carry):
        pl.semaphore_signal(
            barrier, inc=1, device_id=(((xy + o) % NXY) * NZ + z, core), device_id_type=MESH
        )
        return carry

    lax.fori_loop(1, NXY, greet, 0)
    pl.semaphore_signal(barrier, inc=1, device_id=(me, other), device_id_type=MESH)

    for load in small:
        load.wait()
    dest = dest_ref[...]
    shard = jnp.right_shift(dest, 8).astype(F32)
    slot = jnp.bitwise_and(dest, 255).astype(F32)
    by_lane = jnp.broadcast_to(shard, (ROWS, ROWS))
    by_row = by_lane.T
    earlier = (by_lane == by_row) & (iota((ROWS, ROWS), 0) < iota((ROWS, ROWS), 1))
    rank = jnp.sum(jnp.where(earlier, 1.0, 0.0), axis=0, keepdims=True)
    hit = iota((SHARDS, ROWS), 0).astype(F32) == shard
    mine = hit & (rank == core.astype(F32))
    pick = jnp.where(mine, 1.0, 0.0).astype(BF16)
    pair = iota((8, ROWS), 0).astype(F32) == rank
    slots = jnp.where(pair, slot, 0.0).astype(BF16)
    posa_src[...] = mm_nt(slots, jnp.where(hit, 1.0, 0.0).astype(BF16))[0:2, :]
    load_tok.wait()
    gain = gain_ref[...]
    rows = mm(pick, tok[...])
    scale = lax.rsqrt(jnp.sum(rows * rows, axis=-1, keepdims=True) * (1.0 / WIDTH) + 1e-05)
    for j in range(CHUNKS):
        cols = slice(j * 128, (j + 1) * 128)
        stage[pl.ds(j, SHARDS, stride=CHUNKS), :] = rows[:, cols] * scale * gain[:, cols]
    send[...] = stage[...].reshape(SHARDS, CHUNKS, 128).astype(BF16)

    line = iota((256, 256), 0)
    head_at, unit = line // 64, line % 16
    level_at = (line % 64) // 16
    origin = jnp.where(
        level_at == 0, head_at * 16 + unit,
        jnp.where(
            level_at == 1, 64 + (unit // 8) * 32 + head_at * 8 + unit % 8,
            jnp.where(
                level_at == 2, 128 + (unit // 4) * 16 + head_at * 4 + unit % 4,
                192 + (unit // 2) * 8 + head_at * 2 + unit % 2,
            ),
        ),
    )
    line_up[...] = jnp.where(iota((256, 256), 1) == origin, 1.0, 0.0).astype(BF16)

    pl.semaphore_wait(barrier, NZ - 1 + NXY)
    for o in range(1, NZ):
        pl.semaphore_signal(
            go.at[NZ - o], inc=1, device_id=(xy * NZ + (z + o) % NZ, core), device_id_type=MESH
        )

    posa[z] = posa_src[...]
    for o in range(1, NZ):
        remote(
            posa_src, posa.at[z], pos_sem.at[0], pos_sem.at[1], xy * NZ + (z + o) % NZ, core,
        ).start()

    def send_rows(first, wave):
        def body(i, carry):
            at = ((y + i // NX) % NY) * NX + (x + i % NX) % NX
            for oz in wave:
                group = ORDER.index(oz)
                peer = at * NZ + (z + oz) % NZ
                remote(
                    send.at[peer], recv.at[group * NXY + xy], row_send, row_recv.at[group],
                    peer, core,
                ).start()
            return carry

        lax.fori_loop(first, NXY, body, 0)

    pltpu.make_async_copy(send.at[me], recv.at[xy], row_recv.at[0]).start()
    send_rows(1, WAVES[0])
    for wave in WAVES[1:]:
        for oz in wave:
            pl.semaphore_wait(go.at[oz], 1)
        send_rows(0, wave)
    drain(posa.at[pl.ds(0, NZ - 1)], pos_sem.at[1])
    for oz in range(NZ):
        for k in range(2):
            posb_src[k * NZ + oz:k * NZ + oz + 1, :] = posa[oz, k:k + 1, :]
    posb[pl.ds(pl.multiple_of(xy * 16, 16), 16), :] = posb_src[...]

    def send_pos(o, carry):
        remote(
            posb_src, posb.at[pl.ds(pl.multiple_of(xy * 16, 16), 16)], pos_sem.at[2],
            pos_sem.at[3], ((xy + o) % NXY) * NZ + z, core,
        ).start()
        return carry

    lax.fori_loop(1, NXY, send_pos, 0)

    def unpack(group, landed, line):
        part = pl.ds(group * NXY * CHUNKS, NXY * CHUNKS)
        stage[part, :] = (
            landed[group * NXY:(group + 1) * NXY].astype(F32).reshape(NXY * CHUNKS, 128)
        )
        for j in range(CHUNKS):
            xs[line:line + NXY, j * 128:(j + 1) * 128] = (
                stage[pl.ds(group * NXY * CHUNKS + j, NXY, stride=CHUNKS), :].astype(BF16)
            )

    def collect(part):
        first, last = PARTS[part], PARTS[part + 1]
        line = 2 * NXY * first
        for group in range(first, last):
            block = pl.ds(group * NXY, NXY)
            drain(recv.at[block], row_recv.at[group])
            remote(
                recv.at[block], recv_sib.at[block], sib_send, sib_recv.at[group], me, other
            ).start()
            unpack(group, recv, line)
            line += NXY
        for group in range(first, last):
            drain(recv_sib.at[pl.ds(group * NXY, NXY)], sib_recv.at[group])
            unpack(group, recv_sib, line)
            line += NXY

    def span(number):
        return pl.ds(2 * NXY * PARTS[number], 2 * NXY * (PARTS[number + 1] - PARTS[number]))

    def project(part, own, number):
        lines = span(number)
        own[lines, :] = mm(xs[lines, :], wqkv[part]).astype(BF16)

    def send_halo(own, halo, number, send_sem, recv_sem):
        lines = span(number)
        for side, peer in ((1, left), (0, right)):
            remote(
                own.at[lines], halo.at[side, lines], send_sem, recv_sem.at[side, number], peer, core
            ).start()

    last = len(PARTS) - 2
    for number in range(last + 1):
        collect(number)
        if number == 0:
            load_w[1].wait()
            load_w[2].wait()
        project(1, k_own, number)
        send_halo(k_own, k_halo, number, k_send, k_recv)
        project(2, v_own, number)
        if number < last:
            send_halo(v_own, v_halo, number, v_send, v_recv)

    drain(posb.at[pl.ds(0, 240)], pos_sem.at[3])
    pieces = []
    for number in range(last + 1):
        for who in (core, other):
            for oz in ORDER[PARTS[number]:PARTS[number + 1]]:
                pieces.append(posb[pl.ds(who * NZ + (z + NZ - oz) % NZ, NXY, stride=16), :])
    table = jnp.concatenate(pieces, axis=0).astype(BF16)
    my_lane = jnp.where(iota((8, 128), 1) == me, 1.0, 0.0).astype(BF16)
    pos_row = mm_nt(my_lane, table)[0:1, :]
    where_to = jnp.where(iota((ROWS, ROWS), 0).astype(F32) == pos_row, 1.0, 0.0).astype(BF16)
    place[...] = where_to
    seg = seg_ref[...].astype(F32)
    ids_src[...] = mm(jnp.broadcast_to(seg, (8, ROWS)).astype(BF16), where_to)
    for side, peer in ((1, left), (0, right)):
        remote(ids_src, ids_halo.at[side], ids_sem.at[0], ids_sem.at[1], peer, core).start()

    place_int = pos_row.astype(jnp.int32)
    line = iota((128, ROWS), 0)
    spread = jnp.broadcast_to(place_int, (128, ROWS))
    weights = jnp.zeros((128, ROWS), F32)
    start = 0
    for level in range(4):
        count = 16 >> level
        inside = (line >= start) & (line < start + HEADS * count)
        same = jnp.right_shift(spread, 4 + level) == (line - start) % count
        weights = jnp.where(inside & same, 1.0 / (16 << level), weights)
        start += HEADS * count
    pool[...] = weights.astype(BF16)

    own_col = jnp.broadcast_to(seg, (ROWS, ROWS)).T
    bias[:, 0:ROWS] = jnp.where(own_col == ids_src[0:1, :], 0.0, -jnp.inf)

    line = iota((128, 128), 0)
    head_of = jnp.where(
        line < 64, line // 16,
        jnp.where(line < 96, (line - 64) // 8, jnp.where(line < 112, (line - 96) // 4, (line - 112) // 2)),
    )
    for which, own in ((0, k_own), (1, v_own)):
        picked = jnp.zeros((128, 128), F32)
        for half in range(2):
            means = mm(pool[...], own[:, half * 256:(half + 1) * 256])
            for sub in range(2):
                picked = jnp.where(
                    head_of == half * 2 + sub, means[:, sub * 128:(sub + 1) * 128], picked
                )
        crs_src[:, which * 128:(which + 1) * 128] = picked.astype(BF16)
    start = 0
    for level in range(4):
        size = 1 << level
        lines = 64 >> level
        group = me // size
        partner = group + 1 - 2 * (group % 2)
        for i in range(size):
            remote(
                crs_src.at[pl.ds(start, lines)],
                crs.at[pl.ds(pl.multiple_of(64 * level + (me % size) * lines, 8), lines)],
                crs_sem.at[0], crs_sem.at[1], partner * size + i, core,
            ).start()
        start += lines
    send_halo(v_own, v_halo, last, v_send, v_recv)
    remote(
        wout_hbm.at[:, pl.ds(pl.multiple_of(other * 1024, 1024), 1024)], wo_sib,
        wo_sem.at[0], wo_sem.at[1], me, other,
    ).start()

    load_w[0].wait()
    for half in range(2):
        cols = slice(half * 256, (half + 1) * 256)
        q_raw[half] = mm(xs[...], wqkv[0, :, cols]).astype(BF16)
    for half in range(2):
        q_own[half] = mm(place[...], q_raw[half]).astype(BF16)

    def head(ref, h):
        return ref[:, h * 128:(h + 1) * 128]

    def fine(h, keys, mask):
        return mm_nt(q_own[h // 2, :, (h % 2) * 128:(h % 2 + 1) * 128], keys) * SCORE + mask

    for h in range(HEADS):
        score = fine(h, head(k_own, h), bias[:, 0:ROWS])
        best = jnp.max(score, axis=-1, keepdims=True)
        weight = jnp.exp2(score - best)
        tot[h] = jnp.broadcast_to(jnp.sum(weight, axis=-1, keepdims=True), (ROWS, 128))
        top[h] = jnp.broadcast_to(best, (ROWS, 128))
        acc[h] = mm(weight.astype(BF16), head(v_own, h))

    drain(ids_halo, ids_sem.at[1])
    own_col = jnp.broadcast_to(seg, (ROWS, ROWS)).T
    edge = ((me > 0), (me < SHARDS - 1))
    for side in range(2):
        same = own_col == ids_halo[side][0:1, :]
        bias[:, (side + 1) * ROWS:(side + 2) * ROWS] = jnp.where(same & edge[side], 0.0, -jnp.inf)

    for number in range(last + 1):
        for side in range(2):
            drain(k_halo.at[side, span(number)], k_recv.at[side, number])

    for h in range(HEADS):
        scores = [
            fine(h, head(k_halo.at[side], h), bias[:, (side + 1) * ROWS:(side + 2) * ROWS])
            for side in range(2)
        ]
        old = top[h][:, 0:1]
        best = old
        for score in scores:
            best = jnp.maximum(best, jnp.max(score, axis=-1, keepdims=True))
        fade = jnp.exp2(old - best)
        total = tot[h] * fade
        acc[h] = acc[h] * fade
        for side in range(2):
            weight = jnp.exp2(scores[side] - best)
            total = total + jnp.sum(weight, axis=-1, keepdims=True)
            prob[h, side] = weight.astype(BF16)
        tot[h] = total
        top[h] = jnp.broadcast_to(best, (ROWS, 128))

    drain(crs, crs_sem.at[1])
    far[...] = mm(line_up[...], crs[...]).astype(BF16)
    lift = (iota((8, 64), 1) // 16 + 4).astype(F32)[0:1, :]
    for h in range(HEADS):
        score = fine(h, far[h * 64:(h + 1) * 64, 0:128], lift)
        old = top[h][:, 0:1]
        best = jnp.maximum(old, jnp.max(score, axis=-1, keepdims=True))
        fade = jnp.exp2(old - best)
        weight = jnp.exp2(score - best)
        tot[h] = tot[h] * fade + jnp.sum(weight, axis=-1, keepdims=True)
        top[h] = jnp.broadcast_to(fade, (ROWS, 128))
        far_sum[h] = mm(weight.astype(BF16), far[h * 64:(h + 1) * 64, 128:256])

    for number in range(last):
        for side in range(2):
            drain(v_halo.at[side, span(number)], v_recv.at[side, number])
    for h in range(HEADS):
        total = acc[h]
        for side in range(2):
            total = total + mm(prob[h, side, :, 0:128], v_halo[side, 0:128, h * 128:(h + 1) * 128])
        acc[h] = total
    load_wo.wait()
    for side in range(2):
        drain(v_halo.at[side, span(last)], v_recv.at[side, last])
    for half in range(2):
        for h in (half * 2, half * 2 + 1):
            total = acc[h]
            for side in range(2):
                total = total + mm(prob[h, side, :, 128:256], v_halo[side, 128:256, h * 128:(h + 1) * 128])
            total = total * top[h] + far_sum[h]
            at_own[half, :, (h % 2) * 128:(h % 2 + 1) * 128] = (total / tot[h]).astype(BF16)
        remote(
            at_own.at[half], at_sib.at[half], at_sem.at[0], at_sem.at[1 + half], me, other
        ).start()

    for half in range(2):
        lines = slice(half * 256, (half + 1) * 256)
        for part in range(4):
            cols = slice(part * 256, (part + 1) * 256)
            product = mm(at_own[half], wo_own[lines, cols])
            if half == 0:
                sums[:, cols] = product
            else:
                sums[:, cols] = sums[:, cols] + product
    drain(wo_sib, wo_sem.at[1])
    for half in range(2):
        lines = slice(half * 256, (half + 1) * 256)
        drain(at_sib.at[half], at_sem.at[1 + half])
        for part in range(4):
            cols = slice(part * 256, (part + 1) * 256)
            total = sums[:, cols] + mm(at_sib[half], wo_sib[lines, cols])
            if half == 0:
                sums[:, cols] = total
            else:
                out_ref[:, cols] = total.astype(BF16)

    drain(send.at[pl.ds(0, SHARDS - 1)], row_send)
    drain(posa.at[pl.ds(0, NZ - 1)], pos_sem.at[0])
    drain(posb.at[pl.ds(0, 240)], pos_sem.at[2])
    drain(ids_halo, ids_sem.at[0])
    drain(recv, sib_send)
    drain(k_halo, k_send)
    drain(v_halo, v_send)
    drain(crs, crs_sem.at[0])
    drain(wo_sib, wo_sem.at[0])
    drain(at_own, at_sem.at[0])


def shards(tokens, dest, segment_ids, gain, w_qkv, w_out):
    vmem = pl.BlockSpec(memory_space=pltpu.VMEM)
    hbm = pl.BlockSpec(memory_space=pltpu.HBM)
    dma = pltpu.SemaphoreType.DMA
    keep = lambda a: pltpu.with_memory_space_constraint(a, pltpu.HBM)
    V = pltpu.VMEM
    return pl.pallas_call(
        layer,
        out_shape=jax.ShapeDtypeStruct((ROWS, 1024), BF16),
        in_specs=[hbm] * 6,
        out_specs=vmem,
        scratch_shapes=[
            V((1, ROWS), jnp.int32), V((1, ROWS), jnp.int32), V((1, WIDTH), F32),
            V((ROWS, WIDTH), BF16), V((3, WIDTH, GROUP), BF16), V((GROUP, 1024), BF16),
            V((GROUP, 1024), BF16), V((SHARDS * CHUNKS, 128), F32), V((SHARDS, CHUNKS, 128), BF16),
            V((SHARDS, CHUNKS, 128), BF16), V((SHARDS, CHUNKS, 128), BF16), V((ROWS, WIDTH), BF16),
            V((2, 128), F32), V((NZ, 2, 128), F32), V((16, 128), F32), V((256, 128), F32),
            V((ROWS, ROWS), BF16), V((128, ROWS), BF16),
            V((ROWS, GROUP), BF16), V((ROWS, GROUP), BF16), V((2, ROWS, 256), BF16),
            V((2, ROWS, 256), BF16), V((8, ROWS), F32), V((2, 8, ROWS), F32),
            V((2, ROWS, GROUP), BF16), V((2, ROWS, GROUP), BF16),
            V((128, 256), BF16), V((256, 256), BF16), V((256, 256), BF16), V((256, 256), BF16),
            V((ROWS, 3 * ROWS), F32),
            V((HEADS, ROWS, 128), F32), V((HEADS, ROWS, 128), F32), V((HEADS, ROWS, 128), F32),
            V((HEADS, 2, ROWS, ROWS), BF16), V((2, ROWS, 256), BF16), V((2, ROWS, 256), BF16),
            V((ROWS, 1024), F32), V((HEADS, ROWS, 128), F32),
            dma((8,)), dma, dma((NZ,)), dma, dma((NZ,)), pltpu.SemaphoreType.REGULAR((NZ,)),
            dma((4,)), dma((2,)), dma, dma((2, 6)), dma, dma((2, 6)), dma((2,)), dma((2,)), dma((3,)),
        ],
        compiler_params=pltpu.CompilerParams(collective_id=0, has_side_effects=True, vmem_limit_bytes=40 * 2**20),
    )(
        keep(tokens), keep(dest.reshape(1, ROWS)), keep(segment_ids.reshape(1, ROWS)),
        keep(gain.reshape(1, WIDTH)),
        keep(jnp.transpose(w_qkv, (1, 0, 2))), keep(w_out),
    )


def solution(mesh):
    in_specs = (P("seq", None), P("seq"), P("seq"), P(), P(None, None, "head"), P("head", None))
    return jax.shard_map(
        shards, mesh=mesh, in_specs=in_specs, out_specs=P("seq", "head"), check_vma=False
    )
```

```python
import functools
import math

import jax
import jax.numpy as jnp
from jax import lax
from jax.experimental import pallas as pl
from jax.experimental.pallas import tpu as pltpu
from jax.sharding import PartitionSpec as P

MESH = pl.DeviceIdType.MESH
F32 = jnp.float32
BF16 = jnp.bfloat16
NX, NY, NZ = 4, 4, 8
NXY = NX * NY
SHARDS = NXY * NZ
ROWS = 256
WIDTH = 2048
DH = 128
GROUP = 512
HEADS = 4
CHUNKS = WIDTH // 128
SCORE = DH ** (-0.5) * math.log2(math.e)
WAVES = ((0,), (1, 7), (2, 6), (3, 5, 4))
ORDER = tuple(oz for wave in WAVES for oz in wave)
PARTS = (0, 3, 5, 8)


def iota(shape, dim):
    return lax.broadcasted_iota(jnp.int32, shape, dim)


def mm(a, b):
    return jnp.dot(a, b, preferred_element_type=F32)


def mm_nt(a, b):
    return lax.dot_general(a, b, (((1,), (1,)), ((), ())), preferred_element_type=F32)


def layer(
    tok_hbm, dest_hbm, seg_hbm, gain_hbm, wqkv_hbm, wout_hbm, out_ref,
    dest_ref, seg_ref, gain_ref, tok, wqkv, wo_own, wo_sib, stage, send, recv, recv_sib, xs,
    posa_src, posa, posb_src, posb, place, pool,
    k_own, v_own, q_raw, q_own, ids_src, ids_halo, k_halo, v_halo,
    crs_src, crs, line_up, far, bias, top, tot, acc, prob, at_own, at_sib, sums, far_sum,
    load_sem, row_send, row_recv, sib_send, sib_recv, go,
    pos_sem, ids_sem, k_send, k_recv, v_send, v_recv, crs_sem, wo_sem, at_sem,
):
    me = lax.axis_index("seq")
    core = lax.axis_index("head")
    other = 1 - core
    xy, z = me // NZ, me % NZ
    y, x = xy // NX, xy % NX
    left, right = (me + SHARDS - 1) % SHARDS, (me + 1) % SHARDS

    def remote(src, dst, send_sem, recv_sem, seq, head):
        return pltpu.make_async_remote_copy(
            src_ref=src, dst_ref=dst, send_sem=send_sem, recv_sem=recv_sem,
            device_id=(seq, head), device_id_type=MESH,
        )

    def drain(ref, sem):
        pltpu.make_async_copy(ref, ref, sem).wait()

    small = [
        pltpu.make_async_copy(src, dst, load_sem.at[5 + i])
        for i, (src, dst) in enumerate(
            ((dest_hbm, dest_ref), (seg_hbm, seg_ref), (gain_hbm, gain_ref))
        )
    ]
    for load in small:
        load.start()
    load_tok = pltpu.make_async_copy(tok_hbm, tok, load_sem.at[0])
    load_tok.start()
    load_w = [
        pltpu.make_async_copy(wqkv_hbm.at[part], wqkv.at[part], load_sem.at[1 + part])
        for part in range(3)
    ]
    for part in (1, 2, 0):
        load_w[part].start()
    load_wo = pltpu.make_async_copy(
        wout_hbm.at[:, pl.ds(pl.multiple_of(core * 1024, 1024), 1024)], wo_own, load_sem.at[4]
    )
    load_wo.start()

    barrier = pltpu.get_barrier_semaphore()
    for o in range(1, NZ):
        pl.semaphore_signal(
            barrier, inc=1, device_id=(xy * NZ + (z + o) % NZ, core), device_id_type=MESH
        )

    def greet(o, carry):
        pl.semaphore_signal(
            barrier, inc=1, device_id=(((xy + o) % NXY) * NZ + z, core), device_id_type=MESH
        )
        return carry

    lax.fori_loop(1, NXY, greet, 0)
    pl.semaphore_signal(barrier, inc=1, device_id=(me, other), device_id_type=MESH)

    for load in small:
        load.wait()
    dest = dest_ref[...]
    shard = jnp.right_shift(dest, 8).astype(F32)
    slot = jnp.bitwise_and(dest, 255).astype(F32)
    by_lane = jnp.broadcast_to(shard, (ROWS, ROWS))
    by_row = by_lane.T
    earlier = (by_lane == by_row) & (iota((ROWS, ROWS), 0) < iota((ROWS, ROWS), 1))
    rank = jnp.sum(jnp.where(earlier, 1.0, 0.0), axis=0, keepdims=True)
    hit = iota((SHARDS, ROWS), 0).astype(F32) == shard
    mine = hit & (rank == core.astype(F32))
    pick = jnp.where(mine, 1.0, 0.0).astype(BF16)
    pair = iota((8, ROWS), 0).astype(F32) == rank
    slots = jnp.where(pair, slot, 0.0).astype(BF16)
    posa_src[...] = mm_nt(slots, jnp.where(hit, 1.0, 0.0).astype(BF16))[0:2, :]
    load_tok.wait()
    gain = gain_ref[...]
    rows = mm(pick, tok[...])
    scale = lax.rsqrt(jnp.sum(rows * rows, axis=-1, keepdims=True) * (1.0 / WIDTH) + 1e-05)
    for j in range(CHUNKS):
        cols = slice(j * 128, (j + 1) * 128)
        stage[pl.ds(j, SHARDS, stride=CHUNKS), :] = rows[:, cols] * scale * gain[:, cols]
    send[...] = stage[...].reshape(SHARDS, CHUNKS, 128).astype(BF16)

    line = iota((256, 256), 0)
    head_at, unit = line // 64, line % 16
    level_at = (line % 64) // 16
    origin = jnp.where(
        level_at == 0, head_at * 16 + unit,
        jnp.where(
            level_at == 1, 64 + (unit // 8) * 32 + head_at * 8 + unit % 8,
            jnp.where(
                level_at == 2, 128 + (unit // 4) * 16 + head_at * 4 + unit % 4,
                192 + (unit // 2) * 8 + head_at * 2 + unit % 2,
            ),
        ),
    )
    line_up[...] = jnp.where(iota((256, 256), 1) == origin, 1.0, 0.0).astype(BF16)

    pl.semaphore_wait(barrier, NZ - 1 + NXY)
    for o in range(1, NZ):
        pl.semaphore_signal(
            go.at[NZ - o], inc=1, device_id=(xy * NZ + (z + o) % NZ, core), device_id_type=MESH
        )

    posa[z] = posa_src[...]
    for o in range(1, NZ):
        remote(
            posa_src, posa.at[z], pos_sem.at[0], pos_sem.at[1], xy * NZ + (z + o) % NZ, core,
        ).start()

    def send_rows(first, wave):
        def body(i, carry):
            at = ((y + i // NX) % NY) * NX + (x + i % NX) % NX
            for oz in wave:
                group = ORDER.index(oz)
                peer = at * NZ + (z + oz) % NZ
                remote(
                    send.at[peer], recv.at[group * NXY + xy], row_send, row_recv.at[group],
                    peer, core,
                ).start()
            return carry

        lax.fori_loop(first, NXY, body, 0)

    pltpu.make_async_copy(send.at[me], recv.at[xy], row_recv.at[0]).start()
    send_rows(1, WAVES[0])
    for wave in WAVES[1:]:
        for oz in wave:
            pl.semaphore_wait(go.at[oz], 1)
        send_rows(0, wave)
    drain(posa.at[pl.ds(0, NZ - 1)], pos_sem.at[1])
    for oz in range(NZ):
        for k in range(2):
            posb_src[k * NZ + oz:k * NZ + oz + 1, :] = posa[oz, k:k + 1, :]
    posb[pl.ds(pl.multiple_of(xy * 16, 16), 16), :] = posb_src[...]

    def send_pos(o, carry):
        remote(
            posb_src, posb.at[pl.ds(pl.multiple_of(xy * 16, 16), 16)], pos_sem.at[2],
            pos_sem.at[3], ((xy + o) % NXY) * NZ + z, core,
        ).start()
        return carry

    lax.fori_loop(1, NXY, send_pos, 0)

    def unpack(group, landed, line):
        part = pl.ds(group * NXY * CHUNKS, NXY * CHUNKS)
        stage[part, :] = (
            landed[group * NXY:(group + 1) * NXY].astype(F32).reshape(NXY * CHUNKS, 128)
        )
        for j in range(CHUNKS):
            xs[line:line + NXY, j * 128:(j + 1) * 128] = (
                stage[pl.ds(group * NXY * CHUNKS + j, NXY, stride=CHUNKS), :].astype(BF16)
            )

    def collect(part):
        first, last = PARTS[part], PARTS[part + 1]
        line = 2 * NXY * first
        for group in range(first, last):
            block = pl.ds(group * NXY, NXY)
            drain(recv.at[block], row_recv.at[group])
            remote(
                recv.at[block], recv_sib.at[block], sib_send, sib_recv.at[group], me, other
            ).start()
            unpack(group, recv, line)
            line += NXY
        for group in range(first, last):
            drain(recv_sib.at[pl.ds(group * NXY, NXY)], sib_recv.at[group])
            unpack(group, recv_sib, line)
            line += NXY

    def span(number):
        return pl.ds(2 * NXY * PARTS[number], 2 * NXY * (PARTS[number + 1] - PARTS[number]))

    def project(part, own, number):
        lines = span(number)
        own[lines, :] = mm(xs[lines, :], wqkv[part]).astype(BF16)

    def send_halo(own, halo, number, send_sem, recv_sem):
        lines = span(number)
        for side, peer in ((1, left), (0, right)):
            remote(
                own.at[lines], halo.at[side, lines], send_sem, recv_sem.at[side, number], peer, core
            ).start()

    last = len(PARTS) - 2
    for number in range(last + 1):
        collect(number)
        if number == 0:
            load_w[1].wait()
            load_w[2].wait()
        project(1, k_own, number)
        send_halo(k_own, k_halo, number, k_send, k_recv)
        project(2, v_own, number)
        if number < last:
            send_halo(v_own, v_halo, number, v_send, v_recv)

    drain(posb.at[pl.ds(0, 240)], pos_sem.at[3])
    pieces = []
    for number in range(last + 1):
        for who in (core, other):
            for oz in ORDER[PARTS[number]:PARTS[number + 1]]:
                pieces.append(posb[pl.ds(who * NZ + (z + NZ - oz) % NZ, NXY, stride=16), :])
    table = jnp.concatenate(pieces, axis=0).astype(BF16)
    my_lane = jnp.where(iota((8, 128), 1) == me, 1.0, 0.0).astype(BF16)
    pos_row = mm_nt(my_lane, table)[0:1, :]
    where_to = jnp.where(iota((ROWS, ROWS), 0).astype(F32) == pos_row, 1.0, 0.0).astype(BF16)
    place[...] = where_to
    seg = seg_ref[...].astype(F32)
    ids_src[...] = mm(jnp.broadcast_to(seg, (8, ROWS)).astype(BF16), where_to)
    for side, peer in ((1, left), (0, right)):
        remote(ids_src, ids_halo.at[side], ids_sem.at[0], ids_sem.at[1], peer, core).start()

    place_int = pos_row.astype(jnp.int32)
    line = iota((128, ROWS), 0)
    spread = jnp.broadcast_to(place_int, (128, ROWS))
    weights = jnp.zeros((128, ROWS), F32)
    start = 0
    for level in range(4):
        count = 16 >> level
        inside = (line >= start) & (line < start + HEADS * count)
        same = jnp.right_shift(spread, 4 + level) == (line - start) % count
        weights = jnp.where(inside & same, 1.0 / (16 << level), weights)
        start += HEADS * count
    pool[...] = weights.astype(BF16)

    own_col = jnp.broadcast_to(seg, (ROWS, ROWS)).T
    bias[:, 0:ROWS] = jnp.where(own_col == ids_src[0:1, :], 0.0, -jnp.inf)

    line = iota((128, 128), 0)
    head_of = jnp.where(
        line < 64, line // 16,
        jnp.where(line < 96, (line - 64) // 8, jnp.where(line < 112, (line - 96) // 4, (line - 112) // 2)),
    )
    for which, own in ((0, k_own), (1, v_own)):
        picked = jnp.zeros((128, 128), F32)
        for half in range(2):
            means = mm(pool[...], own[:, half * 256:(half + 1) * 256])
            for sub in range(2):
                picked = jnp.where(
                    head_of == half * 2 + sub, means[:, sub * 128:(sub + 1) * 128], picked
                )
        crs_src[:, which * 128:(which + 1) * 128] = picked.astype(BF16)
    start = 0
    for level in range(4):
        size = 1 << level
        lines = 64 >> level
        group = me // size
        partner = group + 1 - 2 * (group % 2)
        for i in range(size):
            remote(
                crs_src.at[pl.ds(start, lines)],
                crs.at[pl.ds(pl.multiple_of(64 * level + (me % size) * lines, 8), lines)],
                crs_sem.at[0], crs_sem.at[1], partner * size + i, core,
            ).start()
        start += lines
    send_halo(v_own, v_halo, last, v_send, v_recv)
    remote(
        wout_hbm.at[:, pl.ds(pl.multiple_of(other * 1024, 1024), 1024)], wo_sib,
        wo_sem.at[0], wo_sem.at[1], me, other,
    ).start()

    load_w[0].wait()
    for half in range(2):
        cols = slice(half * 256, (half + 1) * 256)
        q_raw[half] = mm(xs[...], wqkv[0, :, cols]).astype(BF16)
    for half in range(2):
        q_own[half] = mm(place[...], q_raw[half]).astype(BF16)

    def head(ref, h):
        return ref[:, h * 128:(h + 1) * 128]

    def fine(h, keys, mask):
        return mm_nt(q_own[h // 2, :, (h % 2) * 128:(h % 2 + 1) * 128], keys) * SCORE + mask

    for h in range(HEADS):
        score = fine(h, head(k_own, h), bias[:, 0:ROWS])
        best = jnp.max(score, axis=-1, keepdims=True)
        weight = jnp.exp2(score - best)
        tot[h] = jnp.broadcast_to(jnp.sum(weight, axis=-1, keepdims=True), (ROWS, 128))
        top[h] = jnp.broadcast_to(best, (ROWS, 128))
        acc[h] = mm(weight.astype(BF16), head(v_own, h))

    drain(ids_halo, ids_sem.at[1])
    own_col = jnp.broadcast_to(seg, (ROWS, ROWS)).T
    edge = ((me > 0), (me < SHARDS - 1))
    for side in range(2):
        same = own_col == ids_halo[side][0:1, :]
        bias[:, (side + 1) * ROWS:(side + 2) * ROWS] = jnp.where(same & edge[side], 0.0, -jnp.inf)

    for number in range(last + 1):
        for side in range(2):
            drain(k_halo.at[side, span(number)], k_recv.at[side, number])

    for h in range(HEADS):
        scores = [
            fine(h, head(k_halo.at[side], h), bias[:, (side + 1) * ROWS:(side + 2) * ROWS])
            for side in range(2)
        ]
        old = top[h][:, 0:1]
        best = old
        for score in scores:
            best = jnp.maximum(best, jnp.max(score, axis=-1, keepdims=True))
        fade = jnp.exp2(old - best)
        total = tot[h] * fade
        acc[h] = acc[h] * fade
        for side in range(2):
            weight = jnp.exp2(scores[side] - best)
            total = total + jnp.sum(weight, axis=-1, keepdims=True)
            prob[h, side] = weight.astype(BF16)
        tot[h] = total
        top[h] = jnp.broadcast_to(best, (ROWS, 128))

    drain(crs, crs_sem.at[1])
    far[...] = mm(line_up[...], crs[...]).astype(BF16)
    lift = (iota((8, 64), 1) // 16 + 4).astype(F32)[0:1, :]
    for h in range(HEADS):
        score = fine(h, far[h * 64:(h + 1) * 64, 0:128], lift)
        old = top[h][:, 0:1]
        best = jnp.maximum(old, jnp.max(score, axis=-1, keepdims=True))
        fade = jnp.exp2(old - best)
        weight = jnp.exp2(score - best)
        tot[h] = tot[h] * fade + jnp.sum(weight, axis=-1, keepdims=True)
        top[h] = jnp.broadcast_to(fade, (ROWS, 128))
        far_sum[h] = mm(weight.astype(BF16), far[h * 64:(h + 1) * 64, 128:256])

    for number in range(last):
        for side in range(2):
            drain(v_halo.at[side, span(number)], v_recv.at[side, number])
    for h in range(HEADS):
        total = acc[h]
        for side in range(2):
            total = total + mm(prob[h, side, :, 0:128], v_halo[side, 0:128, h * 128:(h + 1) * 128])
        acc[h] = total
    load_wo.wait()
    for side in range(2):
        drain(v_halo.at[side, span(last)], v_recv.at[side, last])
    for half in range(2):
        for h in (half * 2, half * 2 + 1):
            total = acc[h]
            for side in range(2):
                total = total + mm(prob[h, side, :, 128:256], v_halo[side, 128:256, h * 128:(h + 1) * 128])
            total = total * top[h] + far_sum[h]
            at_own[half, :, (h % 2) * 128:(h % 2 + 1) * 128] = (total / tot[h]).astype(BF16)
            block = pl.ds((h % 2) * 128, 128)
            remote(
                at_own.at[half, :, block], at_sib.at[half, :, block], at_sem.at[0],
                at_sem.at[1 + half], me, other,
            ).start()

    for half in range(2):
        lines = slice(half * 256, (half + 1) * 256)
        for part in range(4):
            cols = slice(part * 256, (part + 1) * 256)
            product = mm(at_own[half], wo_own[lines, cols])
            if half == 0:
                sums[:, cols] = product
            else:
                sums[:, cols] = sums[:, cols] + product
    drain(wo_sib, wo_sem.at[1])
    for half in range(2):
        lines = slice(half * 256, (half + 1) * 256)
        drain(at_sib.at[half], at_sem.at[1 + half])
        for part in range(4):
            cols = slice(part * 256, (part + 1) * 256)
            total = sums[:, cols] + mm(at_sib[half], wo_sib[lines, cols])
            if half == 0:
                sums[:, cols] = total
            else:
                out_ref[:, cols] = total.astype(BF16)

    drain(send.at[pl.ds(0, SHARDS - 1)], row_send)
    drain(posa.at[pl.ds(0, NZ - 1)], pos_sem.at[0])
    drain(posb.at[pl.ds(0, 240)], pos_sem.at[2])
    drain(ids_halo, ids_sem.at[0])
    drain(recv, sib_send)
    drain(k_halo, k_send)
    drain(v_halo, v_send)
    drain(crs, crs_sem.at[0])
    drain(wo_sib, wo_sem.at[0])
    drain(at_own, at_sem.at[0])


def shards(tokens, dest, segment_ids, gain, w_qkv, w_out):
    vmem = pl.BlockSpec(memory_space=pltpu.VMEM)
    hbm = pl.BlockSpec(memory_space=pltpu.HBM)
    dma = pltpu.SemaphoreType.DMA
    keep = lambda a: pltpu.with_memory_space_constraint(a, pltpu.HBM)
    V = pltpu.VMEM
    return pl.pallas_call(
        layer,
        out_shape=jax.ShapeDtypeStruct((ROWS, 1024), BF16),
        in_specs=[hbm] * 6,
        out_specs=vmem,
        scratch_shapes=[
            V((1, ROWS), jnp.int32), V((1, ROWS), jnp.int32), V((1, WIDTH), F32),
            V((ROWS, WIDTH), BF16), V((3, WIDTH, GROUP), BF16), V((GROUP, 1024), BF16),
            V((GROUP, 1024), BF16), V((SHARDS * CHUNKS, 128), F32), V((SHARDS, CHUNKS, 128), BF16),
            V((SHARDS, CHUNKS, 128), BF16), V((SHARDS, CHUNKS, 128), BF16), V((ROWS, WIDTH), BF16),
            V((2, 128), F32), V((NZ, 2, 128), F32), V((16, 128), F32), V((256, 128), F32),
            V((ROWS, ROWS), BF16), V((128, ROWS), BF16),
            V((ROWS, GROUP), BF16), V((ROWS, GROUP), BF16), V((2, ROWS, 256), BF16),
            V((2, ROWS, 256), BF16), V((8, ROWS), F32), V((2, 8, ROWS), F32),
            V((2, ROWS, GROUP), BF16), V((2, ROWS, GROUP), BF16),
            V((128, 256), BF16), V((256, 256), BF16), V((256, 256), BF16), V((256, 256), BF16),
            V((ROWS, 3 * ROWS), F32),
            V((HEADS, ROWS, 128), F32), V((HEADS, ROWS, 128), F32), V((HEADS, ROWS, 128), F32),
            V((HEADS, 2, ROWS, ROWS), BF16), V((2, ROWS, 256), BF16), V((2, ROWS, 256), BF16),
            V((ROWS, 1024), F32), V((HEADS, ROWS, 128), F32),
            dma((8,)), dma, dma((NZ,)), dma, dma((NZ,)), pltpu.SemaphoreType.REGULAR((NZ,)),
            dma((4,)), dma((2,)), dma, dma((2, 6)), dma, dma((2, 6)), dma((2,)), dma((2,)), dma((3,)),
        ],
        compiler_params=pltpu.CompilerParams(collective_id=0, has_side_effects=True, vmem_limit_bytes=40 * 2**20),
    )(
        keep(tokens), keep(dest.reshape(1, ROWS)), keep(segment_ids.reshape(1, ROWS)),
        keep(gain.reshape(1, WIDTH)),
        keep(jnp.transpose(w_qkv, (1, 0, 2))), keep(w_out),
    )


def solution(mesh):
    in_specs = (P("seq", None), P("seq"), P("seq"), P(), P(None, None, "head"), P("head", None))
    return jax.shard_map(
        shards, mesh=mesh, in_specs=in_specs, out_specs=P("seq", "head"), check_vma=False
    )
```
